256 devices in a mesh: grp: 2 (over x_hi), fsdp: 128 (over z, y, x_lo, core).
Axes of the slice: x: 4 (x_hi: 2, x_lo: 2; x = x_hi * 2 + x_lo), y: 4, z: 8, core: 2. Of those that a mesh axis runs over, the one named last changes fastest.
Arguments:
- token_states: bfloat16 [2, 384, 128, 4096], P('grp', 'fsdp'), may hold values from -250 to 250
- token_ids: int32 [2, 384, 128], P('grp', 'fsdp'), may hold values from 0 to 31999, as said below
- master: float32 [2, 4096, 1024], P('grp', 'fsdp'), may hold values from -0.09375 to 0.09375
- gain: float32 [4096], replicated, may hold values from 0.25 to 4.5
- cand_ids: int32 [384, 8], P('fsdp'), may hold values from 0 to 383, all different within a row
- slab_owner: int32 [384], replicated, may hold values from 0 to 127, as said below
Outputs:
- weights_out: float32 [2, 4096, 1024], P('grp', 'fsdp')
The draws below stay inside these ranges and needn't reach their ends.
Inputs may be any that keep to these rules, and one draw needn't show every extreme that they name: `token_ids`: 0 marks padding, which only follows a sequence's tokens; every sequence has 16 or more tokens. `slab_owner`: each fsdp index owns exactly 3 slab rows; the passages of slot 1 on the device with that index are the rows it owns, in increasing order. `cand_ids`: the ids of one row differ, and every slab row is some query's candidate.
All inputs are finite; a program needn't handle non-finite values.
Results may differ from the reference program's by a relative error of at most 0.012.
The reference program's roundings to bfloat16 on the way count: a program that leaves them out, or rounds other values in their place, can miss the bound.
Values may be sent and summed in bfloat16 or wider, within the bound.
A program may use at most 64 MiB of HBM per device.

```python
import math
import jax
import jax.numpy as jnp
from jax import lax

D = 4096
E = 1024
VOCAB = 32000
LEN = 128
CANDS = 8
SEQ_DEV = 3
SEQS = 384
N_FSDP = 128


def draw_token_states(key, part):
    base_key = jax.random.fold_in(key, 11)
    key_base, key_row, key_column = jax.random.split(base_key, 3)
    values = jnp.clip(jax.random.normal(key_base, (2, SEQS, LEN, D), jnp.float32), -4.0, 4.0)
    row_scale = jnp.exp(jax.random.uniform(key_row, (2, SEQS, LEN, 1), jnp.float32, 0.0, math.log(10.0)))
    column_scale = jnp.exp(jax.random.uniform(key_column, (2, 1, 1, D), jnp.float32, math.log(0.5), math.log(5.0)))
    return (values * row_scale * column_scale).astype(jnp.bfloat16)


def draw_gain(key, part):
    gain_key = jax.random.fold_in(key, 23)
    ramp = jnp.arange(D, dtype=jnp.float32) / (D - 1)
    factor = jnp.exp(jax.random.uniform(gain_key, (D,), jnp.float32, -0.3, 0.3))
    return 0.6 * jnp.power(3.0, ramp) * factor


def draw_token_ids(key, part):
    id_key = jax.random.fold_in(key, 37)
    key_length, key_token = jax.random.split(id_key, 2)
    lengths = jax.random.randint(key_length, (2, SEQS, 1), LEN // 8, LEN + 1)
    tokens = jax.random.randint(key_token, (2, SEQS, LEN), 1, VOCAB)
    places = jnp.arange(LEN)[None, None, :]
    return jnp.where(places < lengths, tokens, 0).astype(jnp.int32)


def draw_slab_owner(key, part):
    shuffled = jax.random.permutation(jax.random.fold_in(key, 41), SEQS)
    return (shuffled // SEQ_DEV).astype(jnp.int32)


def levels(rng, dims, cuts, least, top_value):
    loudness = 1.0
    for position, parts in cuts:
        steps = jax.random.uniform(jax.random.fold_in(jax.random.fold_in(rng, 6), position), (parts,), jnp.float32, least / len(cuts), top_value / len(cuts))
        loudness = loudness * jnp.repeat(jnp.exp(steps), dims[position] // parts).reshape((-1,) + (1,) * (len(dims) - 1 - position))
    return loudness


def distinct(rng, rows, amount, top, lift):
    order = jax.random.permutation(jax.random.fold_in(rng, 1), amount)
    boost = order
    for power in range(3):
        boost = boost * boost // amount
    boost = boost * lift // amount
    lots = jax.random.randint(jax.random.fold_in(rng, 2), (rows, amount), 0, 4096) + boost
    sure = jax.random.permutation(jax.random.fold_in(rng, 3), rows)[jnp.arange(amount) % rows]
    lots = jnp.where(jnp.arange(rows)[:, None] == sure[None, :], 1 << 14, lots)
    score = lots * amount + jnp.arange(amount)
    return lax.top_k(score.astype(jnp.int32), top)[1].astype(jnp.int32)


def normal_values(rng, shape, spread, limit, shards=(), kind=jnp.bfloat16):
    entries = jax.random.normal(rng, shape, jnp.float32) * spread
    if len(shards) > 0:
        entries = levels(rng, shape, shards, -0.22, 0.18) * entries
    return jnp.clip(entries, min=-limit, max=limit).astype(kind)


def setup_inputs(seed: int = 0) -> dict:
    streams_of = jax.random.split(jax.random.key(seed), 7)
    token_states = draw_token_states(jax.random.fold_in(streams_of[6], 71), 0)
    token_ids = draw_token_ids(jax.random.fold_in(streams_of[6], 71), 0)
    master = normal_values(streams_of[2], (2, D, E), D ** -0.5, 0.09375, ((0, 2), (1, 128)), jnp.float32)
    gain = draw_gain(jax.random.fold_in(streams_of[6], 71), 0)
    cand_ids = distinct(streams_of[4], SEQS, SEQS, CANDS, 341)
    slab_owner = draw_slab_owner(jax.random.fold_in(streams_of[6], 71), 0)
    return {"token_states": token_states, "token_ids": token_ids, "master": master, "gain": gain, "cand_ids": cand_ids, "slab_owner": slab_owner}


sharpness = 20.0

def normalize_tokens(states, gain):
    states_wide = states.astype(jnp.float32)
    mean_square = lax.optimization_barrier(jnp.mean(states_wide * states_wide, axis=-1, keepdims=True))
    return (states_wide * lax.rsqrt(mean_square + 1e-05) * gain).astype(jnp.bfloat16)

def block_forward(states, token_ids, weight_bf, gain):
    blocks, length, width = states.shape
    normed = normalize_tokens(states, gain).reshape(blocks * length, width)
    hidden = jnp.dot(normed, weight_bf, preferred_element_type=jnp.float32)
    active = jnp.tanh(hidden).reshape(blocks, length, -1)
    valid = (token_ids != 0).astype(jnp.float32)
    counts = lax.optimization_barrier(jnp.sum(valid, axis=1))
    pooled = lax.optimization_barrier(jnp.sum(active * valid[:, :, None], axis=1)) / counts[:, None]
    return (normed, active, valid, counts, pooled)

def encode(states, token_ids, weight_bf, gain):
    grouped = states.reshape(SEQS // 16, 16, LEN, D)
    grouped_ids = token_ids.reshape(SEQS // 16, 16, LEN)

    def one_block(pair):
        return block_forward(pair[0], pair[1], weight_bf, gain)[4]
    pooled = lax.map(one_block, (grouped, grouped_ids))
    return pooled.reshape(SEQS, E)

def unit_rows(pooled):
    mean_square = lax.optimization_barrier(jnp.mean(pooled * pooled, axis=-1, keepdims=True))
    scale = lax.rsqrt(mean_square + 1e-06)
    return (pooled * scale, scale)

def reference(token_states, token_ids, master, gain, cand_ids, slab_owner):
    query_weight = master[0].astype(jnp.bfloat16)
    passage_weight = master[1].astype(jnp.bfloat16)
    query_pool = encode(token_states[0], token_ids[0], query_weight, gain)
    passage_pool = encode(token_states[1], token_ids[1], passage_weight, gain)
    query_unit, query_scale = unit_rows(query_pool)
    passage_unit, passage_scale = unit_rows(passage_pool)
    stored = passage_unit.astype(jnp.bfloat16)
    owners = jnp.arange(N_FSDP, dtype=jnp.int32)
    onehot = (slab_owner[:, None] == owners[None, :]).astype(jnp.int32)
    ranks = lax.optimization_barrier(jnp.sum((jnp.cumsum(onehot, axis=0) - onehot) * onehot, axis=1))
    places = (slab_owner * SEQ_DEV + ranks).astype(jnp.int32)
    chosen = stored[places[cand_ids]].astype(jnp.float32)
    logits = sharpness / E * jnp.einsum('qe,qje->qj', query_unit, chosen, precision=lax.Precision.HIGHEST)
    exponent = jnp.exp(logits)
    probs = exponent / lax.optimization_barrier(jnp.sum(exponent, axis=-1, keepdims=True))
    target = (jnp.arange(CANDS) == 0).astype(jnp.float32)
    logit_grad = probs - target[None, :]
    unit_grad = sharpness / E * jnp.einsum('qj,qje->qe', logit_grad, chosen, precision=lax.Precision.HIGHEST)
    inner = lax.optimization_barrier(jnp.sum(query_pool * unit_grad, axis=-1, keepdims=True))
    pooled_grad = query_scale * unit_grad - query_pool * (query_scale * query_scale * query_scale) * inner / E
    grouped = token_states[0].reshape(SEQS // 16, 16, LEN, D)
    grouped_ids = token_ids[0].reshape(SEQS // 16, 16, LEN)
    grouped_grad = pooled_grad.reshape(SEQS // 16, 16, E)

    def accumulate(running, triple):
        normed, active, valid, counts, pooled = block_forward(triple[0], triple[1], query_weight, gain)
        delta = (valid / counts[:, None])[:, :, None] * triple[2][:, None, :] * (1.0 - active * active)
        delta = delta.astype(jnp.bfloat16).reshape(-1, E)
        return (running + jnp.dot(normed.T, delta, preferred_element_type=jnp.float32), None)
    grad, unused = lax.scan(accumulate, jnp.zeros((D, E), jnp.float32), (grouped, grouped_ids, grouped_grad))
    row_square = lax.optimization_barrier(jnp.mean(grad * grad, axis=1, keepdims=True))
    normalized = grad * lax.rsqrt(row_square + 1e-06)
    copied = lax.optimization_barrier(query_weight).astype(jnp.float32)
    return jnp.stack([normalized, copied])
```

```python
import jax
import jax.numpy as jnp
from jax import lax
from jax.experimental import pallas as pl
from jax.experimental.pallas import tpu as pltpu
from jax.sharding import PartitionSpec as P

MESH = pl.DeviceIdType.MESH
SHARPNESS = 20.0
NZ, NY = 8, 4
BF, F32 = jnp.bfloat16, jnp.float32
OFFS = (0, -1, 1, -2, 2, -3, 3, 4)
RS_OFFS = (4, 3, -3, 2, -2, 1, -1, 0)
J_ORDER = (0, 1, 3, 2)


def body(
    states_hbm, ids_ref, master_ref, gain_ref, owner_ref, cand_s, owner_s, out_ref,
    states, normed, trans, trans_peer, weight, wrecv, act, stage, stored, slab,
    delta, delta_peer, part, total, big_s, big_r, small_s, small_r, piece_s, piece_r, place_s,
    st_sem, ag_s, ag_r, zr_s, zr_r, yr_s, yr_r, fw_s, fw_r, wt_s, wt_r, tp_s, tp_r,
    e1_s, e1_r, e2_s, e2_r, e3_s, e3_r, dl_s, dl_r, bg_ss, bg_rs, sm_ss, sm_rs, pc_ss, pc_rs,
):
    g = lax.axis_index("grp")
    f = lax.axis_index("fsdp")
    c = f % 2
    x = (f // 2) % 2
    y = (f // 4) % NY
    z = f // 16
    tokens, width = states.shape
    emb = weight.shape[-1]

    def dev(zz, yy, xx, cc, gg=None):
        index = (((zz % NZ) * NY + yy % NY) * 2 + xx) * 2 + cc
        return (g if gg is None else gg, index)

    def copy(src, dst, ssem, rsem, to):
        return pltpu.make_async_remote_copy(
            src_ref=src, dst_ref=dst, send_sem=ssem, recv_sem=rsem,
            device_id=to, device_id_type=MESH,
        )

    me = (g, f)
    partner = dev(z, y, x, 1 - c)

    load = pltpu.make_async_copy(states_hbm, states, st_sem)
    load.start()
    weight[z, y, x, c] = master_ref[...].astype(BF)

    barrier = pltpu.get_barrier_semaphore()
    peers = [dev(z, y + dy, (x + dx) % 2, c) for dy in range(NY) for dx in range(2) if dy or dx]
    peers += [dev(z + 1, y, x, c), dev(z - 1, y, x, c), partner]
    peers += [dev(zz, y, x, c, 1 - g) for zz in range(NZ)]
    for peer in peers:
        pl.semaphore_signal(barrier, inc=1, device_id=peer, device_id_type=MESH)
    pl.semaphore_wait(barrier, len(peers))

    def shard(zz, yy, xx, cc):
        return weight.at[zz % NZ, yy % NY, xx, cc]

    def chunk(zz, yy, cc):
        return weight.at[zz % NZ, yy % NY, :, cc]

    def forward(zz, yy, cc):
        k = (zz % NZ) * NY + yy % NY
        ref = chunk(zz, yy, cc)
        copy(ref, ref, fw_s.at[k], fw_r.at[k], partner).start()

    def send_chunk(ref, ssem, rsem, to):
        copy(ref, ref, ssem, rsem, to).start()

    def got(ref, ssem, rsem):
        copy(ref, ref, ssem, rsem, me).wait_recv()

    def sent(ref, ssem, rsem):
        copy(ref, ref, ssem, rsem, me).wait_send()

    own = shard(z, y, x, c)

    def norm_step(i, carry):
        rows = pl.ds(pl.multiple_of(i * 16, 16), 16)
        wide = states[rows, :].astype(F32)
        mean_square = jnp.sum(wide * wide, axis=-1, keepdims=True) * (1.0 / width)
        normed[rows, :] = (wide * lax.rsqrt(mean_square + 1e-05) * gain_ref[...]).astype(BF)
        return carry

    def norm():
        load.wait()
        lax.fori_loop(0, tokens // 16, norm_step, 0)

    def transpose_step(i, carry):
        columns = pl.ds(pl.multiple_of(i * 512, 512), 512)
        turned = jnp.transpose(normed[:, columns])
        trans[i] = turned.reshape(NY, 2, 2, 32, tokens)
        return carry

    def transpose(lo, hi):
        lax.fori_loop(lo, hi, transpose_step, 0)

    trainer = g == 0

    def weight_copy():
        return copy(own, wrecv, wt_s, wt_r, (1 - g, f))

    @pl.when(trainer)
    def _():
        weight_copy().start()

    @pl.when(c == 0)
    def _():
        for dy in range(NY):
            for dx in range(2):
                if dy or dx:
                    k = dy * 2 + dx
                    send_chunk(own, ag_s.at[k], ag_r.at[k], dev(z, y + dy, (x + dx) % 2, 0))
        norm()
        step = (1, -1)
        for j in J_ORDER:
            yj = y + j
            for dx in range(2):
                if j or dx:
                    k = ((-j) % NY) * 2 + dx
                    got(shard(z, yj, (x + dx) % 2, 0), ag_s.at[k], ag_r.at[k])
            for d in range(2):
                send_chunk(chunk(z, yj, 0), zr_s.at[d, 0, j], zr_r.at[d, 0, j], dev(z + step[d], y, x, 0))
            forward(z, yj, 0)
        transpose(0, 2)
        for s in range(2, 5):
            for j in J_ORDER:
                yj = y + j
                for d in range(2):
                    zz = z - step[d] * (s - 1)
                    got(chunk(zz, yj, 0), zr_s.at[d, s - 2, j], zr_r.at[d, s - 2, j])
                    if s < 4 or (j % 2) == d:
                        send_chunk(
                            chunk(zz, yj, 0), zr_s.at[d, s - 1, j], zr_r.at[d, s - 1, j],
                            dev(z + step[d], y, x, 0),
                        )
                    forward(zz, yj, 0)
            transpose(2 * s - 2, 2 * s)
        for j in J_ORDER:
            d = j % 2
            got(chunk(z + 4, y + j, 0), zr_s.at[d, 3, j], zr_r.at[d, 3, j])
            forward(z + 4, y + j, 0)
        for dy in range(NY):
            for dx in range(2):
                if dy or dx:
                    k = dy * 2 + dx
                    sent(own, ag_s.at[k], ag_r.at[k])
        for s in range(1, 5):
            for j in range(NY):
                for d in range(2):
                    if s < 4 or (j % 2) == d:
                        sent(chunk(z, y, 0), zr_s.at[d, s - 1, j], zr_r.at[d, s - 1, j])

    @pl.when(c == 1)
    def _():
        step = (1, -1)
        send_chunk(own, ag_s.at[1], ag_r.at[1], dev(z, y, 1 - x, 1))
        for d in range(2):
            send_chunk(own, zr_s.at[d, 0, 0], zr_r.at[d, 0, 0], dev(z + step[d], y, x, 1))
        norm()

        def spread(k):
            zz = z + OFFS[k]
            for d in range(2):
                send_chunk(chunk(zz, y, 1), yr_s.at[d, 0, k], yr_r.at[d, 0, k], dev(z, y + step[d], x, 1))
            forward(zz, y, 1)

        other = shard(z, y, 1 - x, 1)
        got(other, ag_s.at[1], ag_r.at[1])
        for d in range(2):
            send_chunk(other, zr_s.at[d, 0, 1], zr_r.at[d, 0, 1], dev(z + step[d], y, x, 1))
        spread(0)
        for s in range(2, 5):
            for d in range(2):
                zz = z - step[d] * (s - 1)
                for j in range(2):
                    ref = shard(zz, y, (x + j) % 2, 1)
                    got(ref, zr_s.at[d, s - 2, j], zr_r.at[d, s - 2, j])
                    if s < 4 or j == d:
                        send_chunk(ref, zr_s.at[d, s - 1, j], zr_r.at[d, s - 1, j], dev(z + step[d], y, x, 1))
                spread(2 * (s - 1) - 1 + d)
            transpose(2 * s - 4, 2 * s - 2)
        for j in range(2):
            got(shard(z + 4, y, (x + j) % 2, 1), zr_s.at[j, 3, j], zr_r.at[j, 3, j])
        spread(7)
        for k in range(NZ):
            for d in range(2):
                ref = chunk(z + OFFS[k], y - step[d], 1)
                got(ref, yr_s.at[d, 0, k], yr_r.at[d, 0, k])
                if k % 2 == d:
                    send_chunk(ref, yr_s.at[d, 1, k], yr_r.at[d, 1, k], dev(z, y + step[d], x, 1))
                forward(z + OFFS[k], y - step[d], 1)
            if k == 3:
                transpose(6, 8)
        for k in range(NZ):
            d = k % 2
            got(chunk(z + OFFS[k], y + 2, 1), yr_s.at[d, 1, k], yr_r.at[d, 1, k])
            forward(z + OFFS[k], y + 2, 1)
        sent(own, ag_s.at[1], ag_r.at[1])
        for s in range(1, 5):
            for j in range(2):
                for d in range(2):
                    if s < 4 or j == d:
                        sent(own, zr_s.at[d, s - 1, j], zr_r.at[d, s - 1, j])
        for k in range(NZ):
            for d in range(2):
                sent(chunk(z, y, 1), yr_s.at[d, 0, k], yr_r.at[d, 0, k])
            sent(chunk(z, y, 1), yr_s.at[k % 2, 1, k], yr_r.at[k % 2, 1, k])

    def turned_copy():
        return copy(trans.at[:, :, :, 1 - c], trans_peer, tp_s, tp_r, partner)

    @pl.when(trainer)
    def _():
        turned_copy().start()
        position = (
            lax.broadcasted_iota(jnp.int32, owner_ref.shape, 0) * owner_ref.shape[1]
            + lax.broadcasted_iota(jnp.int32, owner_ref.shape, 1)
        )
        for q in range(3):
            for j in range(8):
                row = cand_s[q, j]
                owner = owner_s[row]
                same = (owner_ref[...] == owner) & (position < row)
                place_s[q * 8 + j] = owner * 3 + jnp.sum(same.astype(jnp.int32))

    def fw_got(k, carry):
        got(weight.at[k // NY, k % NY, :, 1 - c], fw_s.at[k], fw_r.at[k])
        return carry

    lax.fori_loop(0, NZ * NY, fw_got, 0)

    def hidden_step(n, carry):
        columns = pl.ds(pl.multiple_of(n * 256, 256), 256)
        block = weight[:, :, :, :, :, columns].reshape(width, 256)
        hidden = jnp.dot(normed[...], block, preferred_element_type=F32)
        act[:, columns] = jnp.tanh(hidden)
        return carry

    lax.fori_loop(0, emb // 256, hidden_step, 0)

    def fw_sent(k, carry):
        sent(weight.at[k // NY, k % NY, :, c], fw_s.at[k], fw_r.at[k])
        return carry

    lax.fori_loop(0, NZ * NY, fw_sent, 0)

    lanes = emb // 8
    length = tokens // 3
    places = lax.broadcasted_iota(jnp.int32, (length, lanes), 0)
    counts, masks = [], []
    for q in range(3):
        valid = (ids_ref[q : q + 1, :] != 0).astype(jnp.int32)
        count = jnp.sum(valid, axis=1, keepdims=True)
        counts.append(count.astype(F32))
        masks.append(places < count)
        for k in range(8):
            block = act[q * length : (q + 1) * length, k * lanes : (k + 1) * lanes]
            sums = jnp.sum(jnp.where(masks[q], block, 0.0), axis=0, keepdims=True)
            stage[q, k : k + 1, :] = sums / counts[q]

    def full_sum(v):
        return jnp.sum(jnp.sum(v, axis=1, keepdims=True), axis=0, keepdims=True)

    pooled, scales, units = [], [], []
    for q in range(3):
        pool = stage[q]
        scale = lax.rsqrt(full_sum(pool * pool) * (1.0 / emb) + 1e-06)
        pooled.append(pool)
        scales.append(scale)
        units.append(pool * scale)

    def e1(zz):
        return copy(stored, slab.at[z, y, x, c], e1_s.at[zz], e1_r.at[z], dev(zz, y, x, c, 0))

    @pl.when(g == 1)
    def _():
        for q in range(3):
            stored[q] = units[q].astype(BF)
        for zz in range(NZ):
            e1(zz).start()
        for zz in range(NZ):
            e1(zz).wait_send()
        weight_copy().wait_recv()
        out_ref[...] = wrecv[...].astype(F32)

    @pl.when(trainer)
    def _():
        weight_copy().wait_send()
        for zz in range(NZ):
            got(slab.at[zz, y, x, c], e1_s.at[zz], e1_r.at[zz])
        mine = slab.at[:, y, x, c]

        def e2(dy, dx):
            k = dy * 2 + dx
            return copy(mine, mine, e2_s.at[k], e2_r.at[k], dev(z, y + dy, (x + dx) % 2, c))

        def e3(yy, xx, k, cc):
            ref = slab.at[:, yy % NY, xx, cc]
            return copy(ref, ref, e3_s.at[k], e3_r.at[k], partner)

        rels = [(dy, dx) for dy in range(NY) for dx in range(2)]
        for dy, dx in rels:
            if dy or dx:
                e2(dy, dx).start()
        e3(y, x, 0, c).start()
        for dy, dx in rels:
            if dy or dx:
                k = dy * 2 + dx
                yy, xx = y - dy, (x + dx) % 2
                got(slab.at[:, yy % NY, xx, c], e2_s.at[k], e2_r.at[k])
                e3(yy, xx, k, c).start()
        for dy, dx in rels:
            k = dy * 2 + dx
            e3(y - dy, (x + dx) % 2, k, 1 - c).wait_recv()
        for q in range(3):
            rows, exps = [], []
            for j in range(8):
                p = place_s[q * 8 + j]
                o = p // 3
                row = slab[o // 16, (o // 4) % NY, (o // 2) % 2, o % 2, p - o * 3].astype(F32)
                rows.append(row)
                exps.append(jnp.exp(full_sum(units[q] * row) * (SHARPNESS / emb)))
            norm_sum = exps[0]
            for j in range(1, 8):
                norm_sum = norm_sum + exps[j]
            grad = jnp.zeros_like(rows[0])
            for j in range(8):
                weight_j = exps[j] / norm_sum - (1.0 if j == 0 else 0.0)
                grad = grad + weight_j * rows[j]
            grad = grad * (SHARPNESS / emb)
            inner = full_sum(pooled[q] * grad)
            scale = scales[q]
            stage[q] = scale * grad - pooled[q] * (scale * scale * scale) * inner * (1.0 / emb)
        dl = []
        for q in range(3):
            span = slice(q * length, (q + 1) * length)
            for k in range(8):
                cols = slice(k * lanes, (k + 1) * lanes)
                a = act[span, cols]
                base = jnp.where(masks[q], 1.0 / counts[q], 0.0) * stage[q, k : k + 1, :]
                delta[span, cols] = (base * (1.0 - a * a)).astype(BF)
            dl.append(copy(delta.at[span], delta_peer.at[span], dl_s.at[q], dl_r.at[q], partner))
            if q > 0:
                dl[q - 1].start()
        dl[2].start()
        for dy, dx in rels:
            k = dy * 2 + dx
            if k:
                e2(dy, dx).wait_send()
            e3(y - dy, (x + dx) % 2, k, c).wait_send()
        turned_copy().wait_recv()
        for q in range(3):
            dl[q].wait_recv()

        def piece_at(k):
            return piece_s.at[k]

        def unit(u, lhs, lhs_peer):
            value = jnp.dot(lhs.reshape(256, tokens), delta[...], preferred_element_type=F32)
            value = value + jnp.dot(lhs_peer.reshape(256, tokens), delta_peer[...], preferred_element_type=F32)
            part[u] = value.reshape(4, 64, emb)

        def finish(value):
            mean_square = jnp.sum(value * value, axis=1, keepdims=True) * (1.0 / emb)
            out_ref[...] = value * lax.rsqrt(mean_square + 1e-06)

        step = (1, -1)

        @pl.when(c == 0)
        def _():
            def compute(i, carry):
                u = (z + 4 + i) % NZ
                unit(u, trans[u, :, :, 0], trans_peer[u])
                return carry

            def ring(d, s, j):
                k = (s - 1) * 4 + j
                return copy(
                    big_s.at[d, k], big_r.at[d, k], bg_ss.at[d, k], bg_rs.at[d, k],
                    dev(z + step[d], y, x, 0),
                )

            compute(0, 0)
            for j in range(4):
                d = j % 2
                big_s[d, j] = part[(z + 4) % NZ, j].astype(BF)
            for j in range(4):
                ring(j % 2, 1, j).start()
            lax.fori_loop(1, NZ, compute, 0)
            for s in range(2, 5):
                for j in (range(4) if s > 2 else (0, 1, 2, 3)):
                    for d in range(2):
                        k = (s - 1) * 4 + j
                        value = part[(z + step[d] * (5 - s)) % NZ, j]
                        if s > 2 or j % 2 == d:
                            ring(d, s - 1, j).wait_recv()
                            value = value + big_r[d, k - 4].astype(F32)
                        big_s[d, k] = value.astype(BF)
                        ring(d, s, j).start()
            for j in range(4):
                value = part[z, j]
                for d in range(2):
                    ring(d, 4, j).wait_recv()
                    value = value + big_r[d, 12 + j].astype(F32)
                total[j] = value.reshape(2, 32, emb)
                piece_s[2 * j : 2 * j + 2] = value.astype(BF).reshape(2, 32, emb)

            def swap(dy, dx):
                k = dy * 2 + dx
                yy, xx = (y + dy) % NY, (x + dx) % 2
                return copy(
                    piece_s.at[yy * 2 + xx], piece_r.at[k], pc_ss.at[k], pc_rs.at[k], dev(z, yy, xx, 0)
                )

            for dy, dx in rels:
                if dy or dx:
                    swap(dy, dx).start()
            value = total[y, x]
            for dy, dx in rels:
                if dy or dx:
                    swap(dy, dx).wait_recv()
                    value = value + piece_r[dy * 2 + dx].astype(F32)
            finish(value)
            for dy, dx in rels:
                if dy or dx:
                    swap(dy, dx).wait_send()
            for s in range(1, 5):
                for j in range(4):
                    for d in range(2):
                        if s > 1 or j % 2 == d:
                            ring(d, s, j).wait_send()

        @pl.when(c == 1)
        def _():
            def compute(i, carry):
                yy = (y + 2 + i // 2) % NY
                h = i % 2
                half = pl.ds(h * 4, 4)
                unit(yy * 2 + h, trans[half, yy, :, 1], trans_peer[half, yy])
                return carry

            def local(yy, j):
                zz = (z + RS_OFFS[j]) % NZ
                return part[(yy % NY) * 2 + zz // 4, zz % 4]

            def ring(d, s, j):
                k = (s - 1) * 8 + j
                return copy(
                    big_s.at[d, k], big_r.at[d, k], bg_ss.at[d, k], bg_rs.at[d, k],
                    dev(z, y + step[d], x, 1),
                )

            lax.fori_loop(0, 2, compute, 0)
            for j in range(8):
                big_s[j % 2, j] = local(y + 2, j).astype(BF)
            for j in range(8):
                ring(j % 2, 1, j).start()
            lax.fori_loop(2, NZ, compute, 0)
            for j in range(8):
                for d in range(2):
                    value = local(y + step[d], j)
                    if j % 2 == d:
                        ring(d, 1, j).wait_recv()
                        value = value + big_r[d, j].astype(F32)
                    big_s[d, 8 + j] = value.astype(BF)
                    ring(d, 2, j).start()

            def landed(j):
                value = local(y, j)
                for d in range(2):
                    ring(d, 2, j).wait_recv()
                    value = value + big_r[d, 8 + j].astype(F32)
                return value.reshape(2, 32, emb)

            def ring2(d, s, j):
                k = (s - 1) * 2 + j
                return copy(
                    small_s.at[d, k], small_r.at[d, k], sm_ss.at[d, k], sm_rs.at[d, k],
                    dev(z + step[d], y, x, 1),
                )

            value = landed(0)
            for j in range(2):
                small_s[j, j] = value[j].astype(BF)
            for j in range(2):
                ring2(j, 1, j).start()
            for s in range(2, 5):
                for d in range(2):
                    value = landed(2 * s - 3 + d)
                    for j in range(2):
                        k = (s - 1) * 2 + j
                        v = value[j]
                        if s > 2 or j == d:
                            ring2(d, s - 1, j).wait_recv()
                            v = v + small_r[d, k - 2].astype(F32)
                        small_s[d, k] = v.astype(BF)
                        ring2(d, s, j).start()
            value = landed(7)
            for j in range(2):
                v = value[j]
                for d in range(2):
                    ring2(d, 4, j).wait_recv()
                    v = v + small_r[d, 6 + j].astype(F32)
                total[0, j] = v
                piece_s[j] = v.astype(BF)
            last = copy(piece_s.at[1 - x], piece_r.at[1], pc_ss.at[1], pc_rs.at[1], dev(z, y, 1 - x, 1))
            last.start()
            last.wait_recv()
            finish(total[0, x] + piece_r[1].astype(F32))
            last.wait_send()
            for j in range(8):
                ring(j % 2, 1, j).wait_send()
                for d in range(2):
                    ring(d, 2, j).wait_send()
            for s in range(1, 5):
                for j in range(2):
                    for d in range(2):
                        if s > 1 or j == d:
                            ring2(d, s, j).wait_send()

        turned_copy().wait_send()
        for q in range(3):
            dl[q].wait_send()


def shards(token_states, token_ids, master, gain, cand_ids, slab_owner):
    seqs, length, width = token_states.shape[1:]
    tokens = seqs * length
    rows, emb = master.shape[1:]
    vmem = pl.BlockSpec(memory_space=pltpu.VMEM)
    smem = pl.BlockSpec(memory_space=pltpu.SMEM)
    dma = pltpu.SemaphoreType.DMA
    V = pltpu.VMEM
    out = pl.pallas_call(
        body,
        out_shape=jax.ShapeDtypeStruct((rows, emb), F32),
        in_specs=[pl.BlockSpec(memory_space=pl.ANY), vmem, vmem, vmem, vmem, smem, smem],
        out_specs=vmem,
        scratch_shapes=[
            V((tokens, width), BF),
            V((tokens, width), BF),
            V((NZ, NY, 2, 2, rows, tokens), BF),
            V((NZ, NY, 2, rows, tokens), BF),
            V((NZ, NY, 2, 2, rows, emb), BF),
            V((rows, emb), BF),
            V((tokens, emb), F32),
            V((3, 8, emb // 8), F32),
            V((3, 8, emb // 8), BF),
            V((NZ, NY, 2, 2, 3, 8, emb // 8), BF),
            V((tokens, emb), BF),
            V((tokens, emb), BF),
            V((NZ, 4, 64, emb), F32),
            V((4, 2, rows, emb), F32),
            V((2, 16, 64, emb), BF),
            V((2, 16, 64, emb), BF),
            V((2, 8, rows, emb), BF),
            V((2, 8, rows, emb), BF),
            V((8, rows, emb), BF),
            V((8, rows, emb), BF),
            pltpu.SMEM((24,), jnp.int32),
            dma,
            dma((8,)), dma((8,)),
            dma((2, 4, 4)), dma((2, 4, 4)),
            dma((2, 2, 8)), dma((2, 2, 8)),
            dma((32,)), dma((32,)),
            dma, dma,
            dma, dma,
            dma((8,)), dma((8,)),
            dma((8,)), dma((8,)),
            dma((8,)), dma((8,)),
            dma((3,)), dma((3,)),
            dma((2, 16)), dma((2, 16)),
            dma((2, 8)), dma((2, 8)),
            dma((8,)), dma((8,)),
        ],
        compiler_params=pltpu.CompilerParams(
            collective_id=0, has_side_effects=True, vmem_limit_bytes=62 * 1024 * 1024
        ),
    )(
        token_states.reshape(tokens, width),
        token_ids[0],
        master[0],
        gain.reshape(1, width),
        slab_owner.reshape(3, -1),
        cand_ids,
        slab_owner,
    )
    return out[None]


def solution(mesh):
    placed = (
        P("grp", "fsdp", None, None),
        P("grp", "fsdp", None),
        P("grp", "fsdp", None),
        P(),
        P("fsdp", None),
        P(),
    )
    return jax.shard_map(
        shards, mesh=mesh, in_specs=placed, out_specs=P("grp", "fsdp", None), check_vma=False
    )
```

```python
import jax
import jax.numpy as jnp
from jax import lax
from jax.experimental import pallas as pl
from jax.experimental.pallas import tpu as pltpu
from jax.sharding import PartitionSpec as P

MESH = pl.DeviceIdType.MESH
SHARPNESS = 20.0
NZ, NY = 8, 4
BF, F32 = jnp.bfloat16, jnp.float32
OFFS = (0, -1, 1, -2, 2, -3, 3, 4)
RS_OFFS = (4, 3, -3, 2, -2, 1, -1, 0)
J_ORDER = (0, 1, 3, 2)
AG_XL = (1, 3, 2)
RS_XL = (1, 3, 2)
STEP = (1, -1)
NEAR = (0, 1, -1, 2, -2)
FAR = (3, -3, 4)


def units_of(x_last):
    pairs = []
    for j in J_ORDER:
        pairs.append((j, 0))
        if j not in x_last:
            pairs.append((j, 1))
    return pairs


def body(
    states_hbm, master_hbm, gain_hbm, ids_ref, owner_ref, cand_s, owner_s, out_ref,
    states, master, gain, normed, trans, trans_peer, weight, wrecv, act, stage, stored, slab,
    delta, delta_peer, part, total, big_s, big_r, x1_s, x1_r, small_s, small_r, fin_s, fin_r, place_s,
    ld_sem, ay_s, ay_r, xf_s, xf_r, zr_s, zr_r, yr_s, yr_r, fw_s, fw_r, wt_s, wt_r, tp_s, tp_r,
    e1_s, e1_r, e2_s, e2_r, e3_s, e3_r, dl_s, dl_r, bg_ss, bg_rs, xx_ss, xx_rs, sm_ss, sm_rs, fi_ss, fi_rs,
):
    g = lax.axis_index("grp")
    f = lax.axis_index("fsdp")
    c = f % 2
    x = (f // 2) % 2
    y = (f // 4) % NY
    z = f // 16
    tokens, width = states.shape
    emb = weight.shape[-1]

    def dev(zz, yy, xx, cc, gg=None):
        index = (((zz % NZ) * NY + yy % NY) * 2 + xx) * 2 + cc
        return (g if gg is None else gg, index)

    def copy(src, dst, ssem, rsem, to):
        return pltpu.make_async_remote_copy(
            src_ref=src, dst_ref=dst, send_sem=ssem, recv_sem=rsem,
            device_id=to, device_id_type=MESH,
        )

    me = (g, f)
    partner = dev(z, y, x, 1 - c)
    x_next = dev(z, y, 1 - x, c)
    trainer = g == 0

    load_master = pltpu.make_async_copy(master_hbm, master, ld_sem.at[0])
    load_gain = pltpu.make_async_copy(gain_hbm, gain, ld_sem.at[1])
    load = pltpu.make_async_copy(states_hbm, states, ld_sem.at[2])
    load_master.start()
    load_gain.start()
    load.start()

    barrier = pltpu.get_barrier_semaphore()
    peers = [dev(z, y + 1, x, c), dev(z, y + 2, x, c), dev(z, y + 3, x, c)]
    peers += [dev(z + 1, y, x, c), dev(z - 1, y, x, c), x_next, partner, (1 - g, f)]
    for peer in peers:
        pl.semaphore_signal(barrier, inc=1, device_id=peer, device_id_type=MESH)
    load_master.wait()
    weight[z, y, x, c] = master[...].astype(BF)
    pl.semaphore_wait(barrier, len(peers))

    def shard(zz, yy, xx, cc):
        return weight.at[zz % NZ, yy % NY, xx % 2, cc]

    def push(ref, ssem, rsem, to):
        copy(ref, ref, ssem, rsem, to).start()

    def got(ref, ssem, rsem):
        copy(ref, ref, ssem, rsem, me).wait_recv()

    def sent(ref, ssem, rsem):
        copy(ref, ref, ssem, rsem, me).wait_send()

    def forward(zz, yy, xx, cc):
        k = ((zz % NZ) * NY + yy % NY) * 2 + xx % 2
        push(shard(zz, yy, xx, cc), fw_s.at[k], fw_r.at[k], partner)

    own = shard(z, y, x, c)

    def norm_step(i, carry):
        rows = pl.ds(pl.multiple_of(i * 16, 16), 16)
        wide = states[rows, :].astype(F32)
        mean_square = jnp.sum(wide * wide, axis=-1, keepdims=True) * (1.0 / width)
        normed[rows, :] = (wide * lax.rsqrt(mean_square + 1e-05) * gain[...]).astype(BF)
        return carry

    def norm():
        load_gain.wait()
        load.wait()
        lax.fori_loop(0, tokens // 16, norm_step, 0)

    def transpose_step(i, carry):
        columns = pl.ds(pl.multiple_of(i * 512, 512), 512)
        turned = jnp.transpose(normed[:, columns])
        trans[i] = turned.reshape(NY, 2, 2, 32, tokens)
        return carry

    def transpose(lo, hi):
        lax.fori_loop(lo, hi, transpose_step, 0)

    def weight_copy():
        return copy(own, wrecv, wt_s, wt_r, (1 - g, f))

    def weight_start():
        @pl.when(trainer)
        def _():
            weight_copy().start()

    @pl.when(c == 0)
    def _():
        units = units_of(AG_XL)

        def ring(zz, u, s, d):
            j, i = units[u]
            push(
                shard(zz, y + j, x + i, 0), zr_s.at[d, s - 1, u], zr_r.at[d, s - 1, u],
                dev(z + STEP[d], y, x, 0),
            )

        def cross(zz, j):
            k = (zz % NZ) * NY + j
            push(shard(zz, y + j, x, 0), xf_s.at[k], xf_r.at[k], x_next)

        def crossed(zz, j):
            k = (zz % NZ) * NY + j
            got(shard(zz, y + j, x + 1, 0), xf_s.at[k], xf_r.at[k])
            forward(zz, y + j, x + 1, 0)

        for d in range(2):
            ring(z, 0, 1, d)
        cross(z, 0)
        for j in (1, 3, 2):
            push(own, ay_s.at[j], ay_r.at[j], dev(z, y + j, x, 0))
        forward(z, y, x, 0)
        norm()
        crossed(z, 0)
        for d in range(2):
            ring(z, units.index((0, 1)), 1, d)
        for j in (1, 3, 2):
            got(shard(z, y + j, x, 0), ay_s.at[(-j) % NY], ay_r.at[(-j) % NY])
            for d in range(2):
                ring(z, units.index((j, 0)), 1, d)
            cross(z, j)
            forward(z, y + j, x, 0)
        for j in (1, 3, 2):
            if j not in AG_XL:
                crossed(z, j)
                for d in range(2):
                    ring(z, units.index((j, 1)), 1, d)
        transpose(0, 2)

        def serve(zz, first):
            for j in AG_XL:
                crossed(zz, j)

        for s in range(2, 5):
            for u, (j, i) in enumerate(units):
                for d in range(2):
                    zz = z - STEP[d] * (s - 1)
                    got(shard(zz, y + j, x + i, 0), zr_s.at[d, s - 2, u], zr_r.at[d, s - 2, u])
                    if s < 4 or u % 2 == d:
                        ring(zz, u, s, d)
                    if j in AG_XL:
                        cross(zz, j)
                    forward(zz, y + j, x + i, 0)
            if s == 2:
                serve(z, True)
            else:
                for d in range(2):
                    serve(z - STEP[d] * (s - 2), False)
            transpose(2 * s - 2, 2 * s)
        for u, (j, i) in enumerate(units):
            d = u % 2
            got(shard(z + 4, y + j, x + i, 0), zr_s.at[d, 3, u], zr_r.at[d, 3, u])
            if j in AG_XL:
                cross(z + 4, j)
            forward(z + 4, y + j, x + i, 0)
        weight_start()
        for zz in (z - 3, z + 3, z + 4):
            serve(zz, False)
        for j in (1, 3, 2):
            sent(own, ay_s.at[j], ay_r.at[j])
        for u in range(len(units)):
            for s in range(1, 5):
                for d in range(2):
                    if s < 4 or u % 2 == d:
                        sent(own, zr_s.at[d, s - 1, u], zr_r.at[d, s - 1, u])
        for off in range(NZ):
            for j in range(NY):
                if j in AG_XL or off == 0:
                    k = ((z + off) % NZ) * NY + j
                    sent(own, xf_s.at[k], xf_r.at[k])

    @pl.when(c == 1)
    def _():
        def ring(zz, i, s, d):
            push(
                shard(zz, y, x + i, 1), zr_s.at[d, s - 1, i], zr_r.at[d, s - 1, i],
                dev(z + STEP[d], y, x, 1),
            )

        def spread(k, i):
            ref = shard(z + OFFS[k], y, x + i, 1)
            for d in range(2):
                push(ref, yr_s.at[d, 0, 2 * k + i], yr_r.at[d, 0, 2 * k + i], dev(z, y + STEP[d], x, 1))
            forward(z + OFFS[k], y, x + i, 1)

        def serve(k):
            for i in range(2):
                for d in range(2):
                    yy = y - STEP[d]
                    ref = shard(z + OFFS[k], yy, x + i, 1)
                    got(ref, yr_s.at[d, 0, 2 * k + i], yr_r.at[d, 0, 2 * k + i])
                    if i == d:
                        push(ref, yr_s.at[d, 1, k], yr_r.at[d, 1, k], dev(z, y + STEP[d], x, 1))
                    forward(z + OFFS[k], yy, x + i, 1)

        push(own, ay_s.at[0], ay_r.at[0], x_next)
        for d in range(2):
            ring(z, 0, 1, d)
        spread(0, 0)
        norm()
        got(shard(z, y, x + 1, 1), ay_s.at[0], ay_r.at[0])
        for d in range(2):
            ring(z, 1, 1, d)
        spread(0, 1)
        transpose(0, 1)
        for s in range(2, 5):
            for d in range(2):
                zz = z - STEP[d] * (s - 1)
                for i in range(2):
                    got(shard(zz, y, x + i, 1), zr_s.at[d, s - 2, i], zr_r.at[d, s - 2, i])
                    if s < 4 or i == d:
                        ring(zz, i, s, d)
                    spread(2 * s - 3 + d, i)
            for k in (0,) if s == 2 else (2 * s - 5, 2 * s - 4):
                serve(k)
            transpose(2 * s - 3, 2 * s - 1)
        for i in range(2):
            got(shard(z + 4, y, x + i, 1), zr_s.at[i, 3, i], zr_r.at[i, 3, i])
            spread(7, i)
        weight_start()
        transpose(7, 8)
        for k in (5, 6, 7):
            serve(k)
        for k in range(NZ):
            for d in range(2):
                got(shard(z + OFFS[k], y + 2, x + d, 1), yr_s.at[d, 1, k], yr_r.at[d, 1, k])
                forward(z + OFFS[k], y + 2, x + d, 1)
        sent(own, ay_s.at[0], ay_r.at[0])
        for s in range(1, 5):
            for i in range(2):
                for d in range(2):
                    if s < 4 or i == d:
                        sent(own, zr_s.at[d, s - 1, i], zr_r.at[d, s - 1, i])
        for k in range(NZ):
            for d in range(2):
                for i in range(2):
                    sent(own, yr_s.at[d, 0, 2 * k + i], yr_r.at[d, 0, 2 * k + i])
                sent(own, yr_s.at[d, 1, k], yr_r.at[d, 1, k])

    def turned_copy():
        return copy(trans.at[:, :, :, 1 - c], trans_peer, tp_s, tp_r, partner)

    @pl.when(trainer)
    def _():
        turned_copy().start()
        position = (
            lax.broadcasted_iota(jnp.int32, owner_ref.shape, 0) * owner_ref.shape[1]
            + lax.broadcasted_iota(jnp.int32, owner_ref.shape, 1)
        )
        for q in range(3):
            for j in range(8):
                row = cand_s[q, j]
                owner = owner_s[row]
                same = (owner_ref[...] == owner) & (position < row)
                place_s[q * 8 + j] = owner * 3 + jnp.sum(same.astype(jnp.int32))

    def fw_got(k, carry):
        got(weight.at[k // 8, (k // 2) % NY, k % 2, 1 - c], fw_s.at[k], fw_r.at[k])
        return carry

    lax.fori_loop(0, 64, fw_got, 0)

    def hidden_step(n, carry):
        columns = pl.ds(pl.multiple_of(n * 256, 256), 256)
        block = weight[:, :, :, :, :, columns].reshape(width, 256)
        hidden = jnp.dot(normed[...], block, preferred_element_type=F32)
        act[:, columns] = jnp.tanh(hidden)
        return carry

    lax.fori_loop(0, emb // 256, hidden_step, 0)

    def fw_sent(k, carry):
        sent(weight.at[k // 8, (k // 2) % NY, k % 2, c], fw_s.at[k], fw_r.at[k])
        return carry

    lax.fori_loop(0, 64, fw_sent, 0)

    lanes = emb // 8
    length = tokens // 3
    places = lax.broadcasted_iota(jnp.int32, (length, lanes), 0)
    counts, masks = [], []
    for q in range(3):
        valid = (ids_ref[q] != 0).astype(jnp.int32)
        count = jnp.sum(valid, axis=1, keepdims=True)
        counts.append(count.astype(F32))
        masks.append(places < count)
        for k in range(8):
            block = act[q * length : (q + 1) * length, k * lanes : (k + 1) * lanes]
            sums = jnp.sum(jnp.where(masks[q], block, 0.0), axis=0, keepdims=True)
            stage[q, k : k + 1, :] = sums / counts[q]

    def full_sum(v):
        return jnp.sum(jnp.sum(v, axis=1, keepdims=True), axis=0, keepdims=True)

    pooled, scales, units = [], [], []
    for q in range(3):
        pool = stage[q]
        scale = lax.rsqrt(full_sum(pool * pool) * (1.0 / emb) + 1e-06)
        pooled.append(pool)
        scales.append(scale)
        units.append(pool * scale)

    def e1(zz):
        return copy(stored, slab.at[z, y, x, c], e1_s.at[zz % NZ], e1_r.at[z], dev(zz, y, x, c, 0))

    @pl.when(g == 1)
    def _():
        for q in range(3):
            stored[q] = units[q].astype(BF)
        weight_copy().wait_recv()
        for off in (4, 3, -3, 2, -2, 1, -1, 0):
            e1(z + off).start()
        out_ref[...] = wrecv[...].astype(F32)
        for zz in range(NZ):
            e1(zz).wait_send()

    @pl.when(trainer)
    def _():
        rels = [(dy, dx) for dy in range(NY) for dx in range(2)]
        sends = [(2, 0), (2, 1), (1, 0), (3, 0), (1, 1), (3, 1), (0, 1)]

        def e2(b, dy, dx):
            k = b * 8 + dy * 2 + dx
            to = dev(z, y + dy, (x + dx) % 2, c)
            for off in (NEAR, FAR)[b]:
                ref = slab.at[(z + off) % NZ, y, x, c]
                push(ref, e2_s.at[k], e2_r.at[k], to)

        def e3(yy, xx, k, cc):
            ref = slab.at[:, yy % NY, xx, cc]
            return copy(ref, ref, e3_s.at[k], e3_r.at[k], partner)

        for b in range(2):
            for off in (NEAR, FAR)[b]:
                zz = (z + off) % NZ
                got(slab.at[zz, y, x, c], e1_s.at[zz], e1_r.at[zz])
            for dy, dx in sends:
                e2(b, dy, dx)
        e3(y, x, 0, c).start()
        for dy, dx in ((0, 1), (1, 0), (3, 0), (1, 1), (3, 1), (2, 0), (2, 1)):
            k = dy * 2 + dx
            yy, xx = (y - dy) % NY, (x + dx) % 2
            got(slab.at[0:5, yy, xx, c], e2_s.at[k], e2_r.at[k])
            got(slab.at[0:3, yy, xx, c], e2_s.at[8 + k], e2_r.at[8 + k])
            e3(yy, xx, k, c).start()
        for dy, dx in rels:
            k = dy * 2 + dx
            e3(y - dy, (x + dx) % 2, k, 1 - c).wait_recv()
        for q in range(3):
            rows, exps = [], []
            for j in range(8):
                p = place_s[q * 8 + j]
                o = p // 3
                row = slab[o // 16, (o // 4) % NY, (o // 2) % 2, o % 2, p - o * 3].astype(F32)
                rows.append(row)
                exps.append(jnp.exp(full_sum(units[q] * row) * (SHARPNESS / emb)))
            norm_sum = exps[0]
            for j in range(1, 8):
                norm_sum = norm_sum + exps[j]
            grad = jnp.zeros_like(rows[0])
            for j in range(8):
                weight_j = exps[j] / norm_sum - (1.0 if j == 0 else 0.0)
                grad = grad + weight_j * rows[j]
            grad = grad * (SHARPNESS / emb)
            inner = full_sum(pooled[q] * grad)
            scale = scales[q]
            stage[q] = scale * grad - pooled[q] * (scale * scale * scale) * inner * (1.0 / emb)
        dl = []
        for q in range(3):
            span = slice(q * length, (q + 1) * length)
            for k in range(8):
                cols = slice(k * lanes, (k + 1) * lanes)
                a = act[span, cols]
                base = jnp.where(masks[q], 1.0 / counts[q], 0.0) * stage[q, k : k + 1, :]
                delta[span, cols] = (base * (1.0 - a * a)).astype(BF)
            dl.append(copy(delta.at[span], delta_peer.at[span], dl_s.at[q], dl_r.at[q], partner))
            if q > 0:
                dl[q - 1].start()
        dl[2].start()
        for dy, dx in rels:
            k = dy * 2 + dx
            if k:
                sent(slab.at[0:5, y, x, c], e2_s.at[k], e2_r.at[k])
                sent(slab.at[0:3, y, x, c], e2_s.at[8 + k], e2_r.at[8 + k])
            e3(y - dy, (x + dx) % 2, k, c).wait_send()
        weight_copy().wait_send()
        turned_copy().wait_recv()
        for q in range(3):
            dl[q].wait_recv()

        def unit(u, lhs, lhs_peer):
            value = jnp.dot(lhs.reshape(256, tokens), delta[...], preferred_element_type=F32)
            value = value + jnp.dot(lhs_peer.reshape(256, tokens), delta_peer[...], preferred_element_type=F32)
            part[u] = value.reshape(8, 32, emb)

        def finish(value):
            mean_square = jnp.sum(value * value, axis=1, keepdims=True) * (1.0 / emb)
            out_ref[...] = value * lax.rsqrt(mean_square + 1e-06)

        @pl.when(c == 0)
        def _():
            pairs = units_of(RS_XL)
            count = len(pairs)

            def slot(j, i):
                return ((y + j) % NY) * 2 + (x + i) % 2

            def x_first(b, n):
                k = b * 3 + n
                return copy(x1_s.at[k], x1_r.at[k], xx_ss.at[k], xx_rs.at[k], x_next)

            def compute(b, carry):
                odd = b % 2
                off = odd * ((7 - b) // 2) - (1 - odd) * ((8 - b) // 2)
                zz = (z + 16 + off) % NZ
                unit(zz, trans[zz, :, :, 0], trans_peer[zz])
                for n, j in enumerate(RS_XL):
                    x1_s[b * 3 + n] = part[zz, slot(j, 1)].astype(BF)
                return carry

            def compute_send(b, carry):
                compute(b, carry)
                for n in range(len(RS_XL)):
                    x_first(b, n).start()
                return carry

            def ring(d, s, u):
                k = (s - 1) * count + u
                return copy(
                    big_s.at[d, k], big_r.at[d, k], bg_ss.at[d, k], bg_rs.at[d, k],
                    dev(z + STEP[d], y, x, 0),
                )

            def local(b, u):
                j, i = pairs[u]
                value = part[(z + RS_OFFS[b]) % NZ, slot(j, i)]
                if j in RS_XL:
                    n = RS_XL.index(j)
                    x_first(b, n).wait_recv()
                    value = value + x1_r[b * 3 + n].astype(F32)
                return value

            def first(u):
                d = u % 2
                big_s[d, u] = local(0, u).astype(BF)
                ring(d, 1, u).start()

            plain = [u for u, (j, i) in enumerate(pairs) if j not in RS_XL]
            compute_send(0, 0)
            for u in plain:
                first(u)
            lax.fori_loop(1, 4, compute_send, 0)
            for u in range(count):
                if u not in plain:
                    first(u)
            lax.fori_loop(4, NZ, compute_send, 0)
            for s in range(2, 5):
                for u in range(count):
                    for d in range(2):
                        k = (s - 1) * count + u
                        value = local(2 * s - 3 + d, u)
                        if s > 2 or u % 2 == d:
                            ring(d, s - 1, u).wait_recv()
                            value = value + big_r[d, k - count].astype(F32)
                        big_s[d, k] = value.astype(BF)
                        ring(d, s, u).start()

            def last(j, i):
                k = j * 2 + i
                return copy(
                    fin_s.at[k], fin_r.at[k], fi_ss.at[k], fi_rs.at[k], dev(z, y + j, (x + i) % 2, 0)
                )

            for u in list(range(1, count)) + [0]:
                j, i = pairs[u]
                value = local(7, u)
                for d in range(2):
                    ring(d, 4, u).wait_recv()
                    value = value + big_r[d, 3 * count + u].astype(F32)
                if u:
                    fin_s[j * 2 + i] = value.astype(BF)
                    last(j, i).start()
                else:
                    total[0] = value
            value = total[0]
            for j, i in pairs[1:]:
                last(j, i).wait_recv()
                value = value + fin_r[j * 2 + i].astype(F32)
            finish(value)
            for j, i in pairs[1:]:
                last(j, i).wait_send()
            for b in range(NZ):
                for n in range(len(RS_XL)):
                    x_first(b, n).wait_send()
            for s in range(1, 5):
                for u in range(count):
                    for d in range(2):
                        if s > 1 or u % 2 == d:
                            ring(d, s, u).wait_send()

        @pl.when(c == 1)
        def _():
            def compute(i, carry):
                yy = (y + 2 + i // 2) % NY
                h = i % 2
                half = pl.ds(h * 4, 4)
                unit(yy * 2 + h, trans[half, yy, :, 1], trans_peer[half, yy])
                return carry

            def local(yy, j):
                zz = (z + RS_OFFS[j]) % NZ
                return part[(yy % NY) * 2 + zz // 4, pl.ds((zz % 4) * 2, 2)]

            def ring(d, s, j):
                k = (s - 1) * 8 + j
                span = pl.ds(2 * k, 2)
                return copy(
                    big_s.at[d, span], big_r.at[d, span], bg_ss.at[d, k], bg_rs.at[d, k],
                    dev(z, y + STEP[d], x, 1),
                )

            lax.fori_loop(0, 2, compute, 0)
            for j in range(8):
                big_s[j % 2, 2 * j : 2 * j + 2] = local(y + 2, j).astype(BF)
                ring(j % 2, 1, j).start()
            lax.fori_loop(2, NZ, compute, 0)
            for j in range(8):
                for d in range(2):
                    value = local(y + STEP[d], j)
                    if j % 2 == d:
                        ring(d, 1, j).wait_recv()
                        value = value + big_r[d, 2 * j : 2 * j + 2].astype(F32)
                    big_s[d, 16 + 2 * j : 18 + 2 * j] = value.astype(BF)
                    ring(d, 2, j).start()

            def landed(j):
                value = local(y, j)
                for d in range(2):
                    ring(d, 2, j).wait_recv()
                    value = value + big_r[d, 16 + 2 * j : 18 + 2 * j].astype(F32)
                return value

            def ring2(d, s, j):
                k = (s - 1) * 2 + j
                return copy(
                    small_s.at[d, k], small_r.at[d, k], sm_ss.at[d, k], sm_rs.at[d, k],
                    dev(z + STEP[d], y, x, 1),
                )

            value = landed(0)
            for j in range(2):
                small_s[j, j] = value[j].astype(BF)
            for j in range(2):
                ring2(j, 1, j).start()
            for s in range(2, 5):
                for d in range(2):
                    value = landed(2 * s - 3 + d)
                    for j in range(2):
                        k = (s - 1) * 2 + j
                        v = value[j]
                        if s > 2 or j == d:
                            ring2(d, s - 1, j).wait_recv()
                            v = v + small_r[d, k - 2].astype(F32)
                        small_s[d, k] = v.astype(BF)
                        ring2(d, s, j).start()
            value = landed(7)
            for j in range(2):
                v = value[j]
                for d in range(2):
                    ring2(d, 4, j).wait_recv()
                    v = v + small_r[d, 6 + j].astype(F32)
                total[j] = v
                fin_s[j] = v.astype(BF)
            last = copy(fin_s.at[1 - x], fin_r.at[1], fi_ss.at[1], fi_rs.at[1], x_next)
            last.start()
            last.wait_recv()
            finish(total[x] + fin_r[1].astype(F32))
            last.wait_send()
            for j in range(8):
                ring(j % 2, 1, j).wait_send()
                for d in range(2):
                    ring(d, 2, j).wait_send()
            for s in range(1, 5):
                for j in range(2):
                    for d in range(2):
                        if s > 1 or j == d:
                            ring2(d, s, j).wait_send()

        turned_copy().wait_send()
        for q in range(3):
            dl[q].wait_send()


def shards(token_states, token_ids, master, gain, cand_ids, slab_owner):
    seqs, length, width = token_states.shape[1:]
    tokens = seqs * length
    rows, emb = master.shape[1:]
    vmem = pl.BlockSpec(memory_space=pltpu.VMEM)
    smem = pl.BlockSpec(memory_space=pltpu.SMEM)
    hbm = pl.BlockSpec(memory_space=pl.ANY)
    dma = pltpu.SemaphoreType.DMA
    V = pltpu.VMEM
    out = pl.pallas_call(
        body,
        out_shape=jax.ShapeDtypeStruct((rows, emb), F32),
        in_specs=[hbm, hbm, hbm, vmem, vmem, smem, smem],
        out_specs=vmem,
        scratch_shapes=[
            V((tokens, width), BF),
            V((rows, emb), F32),
            V((1, width), F32),
            V((tokens, width), BF),
            V((NZ, NY, 2, 2, rows, tokens), BF),
            V((NZ, NY, 2, rows, tokens), BF),
            V((NZ, NY, 2, 2, rows, emb), BF),
            V((rows, emb), BF),
            V((tokens, emb), F32),
            V((3, 8, emb // 8), F32),
            V((3, 8, emb // 8), BF),
            V((NZ, NY, 2, 2, 3, 8, emb // 8), BF),
            V((tokens, emb), BF),
            V((tokens, emb), BF),
            V((NZ, 8, rows, emb), F32),
            V((2, rows, emb), F32),
            V((2, 32, rows, emb), BF),
            V((2, 32, rows, emb), BF),
            V((24, rows, emb), BF),
            V((24, rows, emb), BF),
            V((2, 8, rows, emb), BF),
            V((2, 8, rows, emb), BF),
            V((8, rows, emb), BF),
            V((8, rows, emb), BF),
            pltpu.SMEM((24,), jnp.int32),
            dma((3,)),
            dma((4,)), dma((4,)),
            dma((32,)), dma((32,)),
            dma((2, 4, 6)), dma((2, 4, 6)),
            dma((2, 2, 16)), dma((2, 2, 16)),
            dma((64,)), dma((64,)),
            dma, dma,
            dma, dma,
            dma((8,)), dma((8,)),
            dma((16,)), dma((16,)),
            dma((8,)), dma((8,)),
            dma((3,)), dma((3,)),
            dma((2, 24)), dma((2, 24)),
            dma((24,)), dma((24,)),
            dma((2, 8)), dma((2, 8)),
            dma((8,)), dma((8,)),
        ],
        compiler_params=pltpu.CompilerParams(
            collective_id=0, has_side_effects=True, vmem_limit_bytes=62 * 1024 * 1024
        ),
    )(
        token_states.reshape(tokens, width),
        master[0],
        gain.reshape(1, width),
        token_ids.reshape(seqs, 1, length),
        slab_owner.reshape(3, -1),
        cand_ids,
        slab_owner,
    )
    return out[None]


def solution(mesh):
    placed = (
        P("grp", "fsdp", None, None),
        P("grp", "fsdp", None),
        P("grp", "fsdp", None),
        P(),
        P("fsdp", None),
        P(),
    )
    return jax.shard_map(
        shards, mesh=mesh, in_specs=placed, out_specs=P("grp", "fsdp", None), check_vma=False
    )
```

```python
import jax
import jax.numpy as jnp
from jax import lax
from jax.experimental import pallas as pl
from jax.experimental.pallas import tpu as pltpu
from jax.sharding import PartitionSpec as P

MESH = pl.DeviceIdType.MESH
SHARPNESS = 20.0
NZ, NY = 8, 4
BF, F32 = jnp.bfloat16, jnp.float32
OFFS = (0, -1, 1, -2, 2, -3, 3, 4)
RS_OFFS = (4, 3, -3, 2, -2, 1, -1, 0)
J_ORDER = (0, 1, 3, 2)
AG_XL = (1, 3, 2)
RS_XL = (1, 3, 2)
STEP = (1, -1)
NEAR = (0, 1, -1, 2, -2)
FAR = (3, -3, 4)


def units_of(x_last):
    pairs = []
    for j in J_ORDER:
        pairs.append((j, 0))
        if j not in x_last:
            pairs.append((j, 1))
    return pairs


def body(
    states_hbm, master_hbm, gain_hbm, ids_ref, owner_ref, cand_s, owner_s, out_ref,
    states, master, gain, normed, trans, trans_peer, weight, wrecv, act, stage, stored, slab,
    delta, delta_peer, part, total, big_s, big_r, x1_s, x1_r, small_s, small_r, fin_s, fin_r, place_s,
    ld_sem, ag_s, ag_r, fw_s, fw_r, wt_s, wt_r, tp_s, tp_r,
    e1_s, e1_r, e2_s, e2_r, e3_s, e3_r, dl_s, dl_r, rs_s, rs_r,
):
    g = lax.axis_index("grp")
    f = lax.axis_index("fsdp")
    c = f % 2
    x = (f // 2) % 2
    y = (f // 4) % NY
    z = f // 16
    tokens, width = states.shape
    emb = weight.shape[-1]

    def dev(zz, yy, xx, cc, gg=None):
        index = (((zz % NZ) * NY + yy % NY) * 2 + xx) * 2 + cc
        return (g if gg is None else gg, index)

    def copy(src, dst, ssem, rsem, to):
        return pltpu.make_async_remote_copy(
            src_ref=src, dst_ref=dst, send_sem=ssem, recv_sem=rsem,
            device_id=to, device_id_type=MESH,
        )

    me = (g, f)
    partner = dev(z, y, x, 1 - c)
    x_next = dev(z, y, 1 - x, c)
    trainer = g == 0

    load_master = pltpu.make_async_copy(master_hbm, master, ld_sem.at[0])
    load_gain = pltpu.make_async_copy(gain_hbm, gain, ld_sem.at[1])
    load = pltpu.make_async_copy(states_hbm, states, ld_sem.at[2])
    load_master.start()
    load_gain.start()
    load.start()

    barrier = pltpu.get_barrier_semaphore()
    peers = [dev(z, y + 1, x, c), dev(z, y + 2, x, c), dev(z, y + 3, x, c)]
    peers += [dev(z + 1, y, x, c), dev(z - 1, y, x, c), x_next, partner, (1 - g, f)]
    for peer in peers:
        pl.semaphore_signal(barrier, inc=1, device_id=peer, device_id_type=MESH)
    load_master.wait()
    weight[z, y, x, c] = master[...].astype(BF)
    pl.semaphore_wait(barrier, len(peers))

    def shard(zz, yy, xx, cc):
        return weight.at[zz % NZ, yy % NY, xx % 2, cc]

    def push(ref, ssem, rsem, to):
        copy(ref, ref, ssem, rsem, to).start()

    def got(ref, ssem, rsem):
        copy(ref, ref, ssem, rsem, me).wait_recv()

    def sent(ref, ssem, rsem):
        copy(ref, ref, ssem, rsem, me).wait_send()

    def forward(zz, yy, xx, cc):
        push(shard(zz, yy, xx, cc), fw_s, fw_r, partner)

    own = shard(z, y, x, c)

    def norm_step(i, carry):
        rows = pl.ds(pl.multiple_of(i * 16, 16), 16)
        wide = states[rows, :].astype(F32)
        mean_square = jnp.sum(wide * wide, axis=-1, keepdims=True) * (1.0 / width)
        normed[rows, :] = (wide * lax.rsqrt(mean_square + 1e-05) * gain[...]).astype(BF)
        return carry

    def norm():
        load_gain.wait()
        load.wait()
        lax.fori_loop(0, tokens // 16, norm_step, 0)

    def transpose_step(i, carry):
        columns = pl.ds(pl.multiple_of(i * 512, 512), 512)
        turned = jnp.transpose(normed[:, columns])
        trans[i] = turned.reshape(NY, 2, 2, 32, tokens)
        return carry

    def transpose(lo, hi):
        lax.fori_loop(lo, hi, transpose_step, 0)

    def weight_copy():
        return copy(own, wrecv, wt_s, wt_r, (1 - g, f))

    def weight_start():
        @pl.when(trainer)
        def _():
            weight_copy().start()

    @pl.when(c == 0)
    def _():
        units = units_of(AG_XL)

        def ring(zz, u, s, d):
            j, i = units[u]
            push(shard(zz, y + j, x + i, 0), ag_s, ag_r.at[place(d, s, u)], dev(z + STEP[d], y, x, 0))

        def place(d, s, u):
            n = len(units)
            return (s - 1) * 2 * n + d * n + u if s < 4 else 6 * n + u

        base = 7 * len(units)

        def spot(k, j):
            return base + (0 if j == 0 else 1 + k * len(AG_XL) + AG_XL.index(j))

        def cross(k, j):
            push(shard(z + OFFS[k], y + j, x, 0), ag_s, ag_r.at[spot(k, j)], x_next)

        def crossed(k, j):
            got(shard(z + OFFS[k], y + j, x + 1, 0), ag_s, ag_r.at[spot(k, j)])
            forward(z + OFFS[k], y + j, x + 1, 0)

        side = base + 1 + NZ * len(AG_XL)

        for d in range(2):
            ring(z, 0, 1, d)
        cross(0, 0)
        for j in (1, 3, 2):
            push(own, ag_s, ag_r.at[side + j - 1], dev(z, y + j, x, 0))
        forward(z, y, x, 0)
        norm()
        crossed(0, 0)
        for d in range(2):
            ring(z, units.index((0, 1)), 1, d)
        for j in (1, 3, 2):
            got(shard(z, y + j, x, 0), ag_s, ag_r.at[side + (-j) % NY - 1])
            for d in range(2):
                ring(z, units.index((j, 0)), 1, d)
            cross(0, j)
            forward(z, y + j, x, 0)
        transpose(0, 2)

        def serve(k):
            for j in AG_XL:
                crossed(k, j)

        for s in range(2, 5):
            for u, (j, i) in enumerate(units):
                for d in range(2):
                    zz = z - STEP[d] * (s - 1)
                    got(shard(zz, y + j, x + i, 0), ag_s, ag_r.at[place(d, s - 1, u)])
                    if s < 4 or u % 2 == d:
                        ring(zz, u, s, d)
                    if j in AG_XL:
                        cross(2 * s - 3 + d, j)
                    forward(zz, y + j, x + i, 0)
            for k in (0,) if s == 2 else (2 * s - 5, 2 * s - 4):
                serve(k)
            transpose(2 * s - 2, 2 * s)
        for u, (j, i) in enumerate(units):
            got(shard(z + 4, y + j, x + i, 0), ag_s, ag_r.at[place(u % 2, 4, u)])
            if j in AG_XL:
                cross(7, j)
            forward(z + 4, y + j, x + i, 0)
        weight_start()
        for k in (5, 6, 7):
            serve(k)
        sent(big_s.at[pl.ds(0, 7 * len(units) + 1 + NZ * len(AG_XL) + 3)], ag_s, ag_r.at[0])

    @pl.when(c == 1)
    def _():
        def ring(zz, i, s, d):
            push(shard(zz, y, x + i, 1), ag_s, ag_r.at[place(d, s, i)], dev(z + STEP[d], y, x, 1))

        def place(d, s, i):
            return (s - 1) * 4 + d * 2 + i if s < 4 else 12 + i

        def near(d, k, i):
            return 14 + d * 16 + 2 * k + i

        def far(d, k):
            return 46 + d * 8 + k

        def spread(k, i):
            ref = shard(z + OFFS[k], y, x + i, 1)
            for d in range(2):
                push(ref, ag_s, ag_r.at[near(d, k, i)], dev(z, y + STEP[d], x, 1))
            forward(z + OFFS[k], y, x + i, 1)

        def serve(k):
            for i in range(2):
                for d in range(2):
                    yy = y - STEP[d]
                    ref = shard(z + OFFS[k], yy, x + i, 1)
                    got(ref, ag_s, ag_r.at[near(d, k, i)])
                    if i == d:
                        push(ref, ag_s, ag_r.at[far(d, k)], dev(z, y + STEP[d], x, 1))
                    forward(z + OFFS[k], yy, x + i, 1)

        push(own, ag_s, ag_r.at[62], x_next)
        for d in range(2):
            ring(z, 0, 1, d)
        spread(0, 0)
        norm()
        got(shard(z, y, x + 1, 1), ag_s, ag_r.at[62])
        for d in range(2):
            ring(z, 1, 1, d)
        spread(0, 1)
        transpose(0, 1)
        for s in range(2, 5):
            for d in range(2):
                zz = z - STEP[d] * (s - 1)
                for i in range(2):
                    got(shard(zz, y, x + i, 1), ag_s, ag_r.at[place(d, s - 1, i)])
                    if s < 4 or i == d:
                        ring(zz, i, s, d)
                    spread(2 * s - 3 + d, i)
            for k in (0,) if s == 2 else (2 * s - 5, 2 * s - 4):
                serve(k)
            transpose(2 * s - 3, 2 * s - 1)
        for i in range(2):
            got(shard(z + 4, y, x + i, 1), ag_s, ag_r.at[place(i, 4, i)])
            spread(7, i)
        weight_start()
        transpose(7, 8)
        for k in (5, 6, 7):
            serve(k)
        for k in range(NZ):
            for d in range(2):
                got(shard(z + OFFS[k], y + 2, x + d, 1), ag_s, ag_r.at[far(d, k)])
                forward(z + OFFS[k], y + 2, x + d, 1)
        sent(big_s.at[pl.ds(0, 63)], ag_s, ag_r.at[0])

    def turned_copy():
        return copy(trans.at[:, :, :, 1 - c], trans_peer, tp_s, tp_r, partner)

    @pl.when(trainer)
    def _():
        turned_copy().start()
        position = (
            lax.broadcasted_iota(jnp.int32, owner_ref.shape, 0) * owner_ref.shape[1]
            + lax.broadcasted_iota(jnp.int32, owner_ref.shape, 1)
        )
        for q in range(3):
            for j in range(8):
                row = cand_s[q, j]
                owner = owner_s[row]
                same = (owner_ref[...] == owner) & (position < row)
                place_s[q * 8 + j] = owner * 3 + jnp.sum(same.astype(jnp.int32))

    got(weight.at[:, :, :, 1 - c], fw_s, fw_r)

    def hidden_step(n, carry):
        columns = pl.ds(pl.multiple_of(n * 256, 256), 256)
        block = weight[:, :, :, :, :, columns].reshape(width, 256)
        hidden = jnp.dot(normed[...], block, preferred_element_type=F32)
        act[:, columns] = jnp.tanh(hidden)
        return carry

    lax.fori_loop(0, emb // 256, hidden_step, 0)

    sent(weight.at[:, :, :, c], fw_s, fw_r)

    lanes = emb // 8
    length = tokens // 3
    places = lax.broadcasted_iota(jnp.int32, (length, lanes), 0)
    counts, masks = [], []
    for q in range(3):
        valid = (ids_ref[q] != 0).astype(jnp.int32)
        count = jnp.sum(valid, axis=1, keepdims=True)
        counts.append(count.astype(F32))
        masks.append(places < count)
        for k in range(8):
            block = act[q * length : (q + 1) * length, k * lanes : (k + 1) * lanes]
            sums = jnp.sum(jnp.where(masks[q], block, 0.0), axis=0, keepdims=True)
            stage[q, k : k + 1, :] = sums / counts[q]

    def full_sum(v):
        return jnp.sum(jnp.sum(v, axis=1, keepdims=True), axis=0, keepdims=True)

    pooled, scales, units = [], [], []
    for q in range(3):
        pool = stage[q]
        scale = lax.rsqrt(full_sum(pool * pool) * (1.0 / emb) + 1e-06)
        pooled.append(pool)
        scales.append(scale)
        units.append(pool * scale)

    @pl.when(g == 1)
    def _():
        for q in range(3):
            stored[q] = units[q].astype(BF)
        weight_copy().wait_recv()
        for b in (1, 0):
            for off in (NEAR, FAR)[b]:
                to = dev(z + off, y, x, c, 0)
                copy(stored, slab.at[z, y, x, c], e1_s, e1_r.at[b], to).start()
        out_ref[...] = wrecv[...].astype(F32)
        sent(slab.at[:, 0, 0, 0], e1_s, e1_r.at[0])

    @pl.when(trainer)
    def _():
        sends = [(2, 0), (2, 1), (1, 0), (3, 0), (1, 1), (3, 1), (0, 1)]

        def e2(b, dy, dx):
            to = dev(z, y + dy, (x + dx) % 2, c)
            for off in (NEAR, FAR)[b]:
                push(slab.at[(z + off) % NZ, y, x, c], e2_s, e2_r.at[dy * 2 + dx], to)

        def e3(yy, xx):
            push(slab.at[:, yy % NY, xx, c], e3_s, e3_r, partner)

        for b in range(2):
            got(slab.at[0 : len((NEAR, FAR)[b]), y, x, c], e1_s, e1_r.at[b])
            for dy, dx in sends:
                e2(b, dy, dx)
        e3(y, x)
        for dy, dx in ((0, 1), (1, 0), (3, 0), (1, 1), (3, 1), (2, 0), (2, 1)):
            yy, xx = (y - dy) % NY, (x + dx) % 2
            got(slab.at[:, yy, xx, c], e2_s, e2_r.at[dy * 2 + dx])
            e3(yy, xx)
        got(slab.at[:, :, :, 1 - c], e3_s, e3_r)
        for q in range(3):
            rows, exps = [], []
            for j in range(8):
                p = place_s[q * 8 + j]
                o = p // 3
                row = slab[o // 16, (o // 4) % NY, (o // 2) % 2, o % 2, p - o * 3].astype(F32)
                rows.append(row)
                exps.append(jnp.exp(full_sum(units[q] * row) * (SHARPNESS / emb)))
            norm_sum = exps[0]
            for j in range(1, 8):
                norm_sum = norm_sum + exps[j]
            grad = jnp.zeros_like(rows[0])
            for j in range(8):
                weight_j = exps[j] / norm_sum - (1.0 if j == 0 else 0.0)
                grad = grad + weight_j * rows[j]
            grad = grad * (SHARPNESS / emb)
            inner = full_sum(pooled[q] * grad)
            scale = scales[q]
            stage[q] = scale * grad - pooled[q] * (scale * scale * scale) * inner * (1.0 / emb)
        dl = []
        for q in range(3):
            span = slice(q * length, (q + 1) * length)
            for k in range(8):
                cols = slice(k * lanes, (k + 1) * lanes)
                a = act[span, cols]
                base = jnp.where(masks[q], 1.0 / counts[q], 0.0) * stage[q, k : k + 1, :]
                delta[span, cols] = (base * (1.0 - a * a)).astype(BF)
            dl.append(copy(delta.at[span], delta_peer.at[span], dl_s, dl_r, partner))
            if q > 0:
                dl[q - 1].start()
        dl[2].start()
        sent(slab.at[0:7, :, :, 0], e2_s, e2_r.at[0])
        sent(slab.at[:, :, :, c], e3_s, e3_r)
        weight_copy().wait_send()
        turned_copy().wait_recv()
        got(delta, dl_s, dl_r)

        def unit(u, lhs, lhs_peer):
            value = jnp.dot(lhs.reshape(256, tokens), delta[...], preferred_element_type=F32)
            value = value + jnp.dot(lhs_peer.reshape(256, tokens), delta_peer[...], preferred_element_type=F32)
            part[u] = value.reshape(8, 32, emb)

        def finish(value):
            mean_square = jnp.sum(value * value, axis=1, keepdims=True) * (1.0 / emb)
            out_ref[...] = value * lax.rsqrt(mean_square + 1e-06)

        @pl.when(c == 0)
        def _():
            pairs = units_of(RS_XL)
            count = len(pairs)

            def slot(j, i):
                return ((y + j) % NY) * 2 + (x + i) % 2

            def x_first(b, n):
                k = b * 3 + n
                return copy(x1_s.at[k], x1_r.at[k], rs_s, rs_r.at[k], x_next)

            def compute(b, carry):
                odd = b % 2
                off = odd * ((7 - b) // 2) - (1 - odd) * ((8 - b) // 2)
                zz = (z + 16 + off) % NZ
                unit(zz, trans[zz, :, :, 0], trans_peer[zz])
                for n, j in enumerate(RS_XL):
                    x1_s[b * 3 + n] = part[zz, slot(j, 1)].astype(BF)
                return carry

            def compute_send(b, carry):
                compute(b, carry)
                for n in range(len(RS_XL)):
                    x_first(b, n).start()
                return carry

            def ring(d, s, u):
                k = spot(d, s, u)
                return copy(big_s.at[k], big_r.at[k], rs_s, rs_r.at[24 + k], dev(z + STEP[d], y, x, 0))

            def spot(d, s, u):
                return u if s == 1 else count + (s - 2) * 2 * count + d * count + u

            def local(b, u):
                j, i = pairs[u]
                value = part[(z + RS_OFFS[b]) % NZ, slot(j, i)]
                if j in RS_XL:
                    n = RS_XL.index(j)
                    x_first(b, n).wait_recv()
                    value = value + x1_r[b * 3 + n].astype(F32)
                return value

            def first(u):
                d = u % 2
                big_s[spot(d, 1, u)] = local(0, u).astype(BF)
                ring(d, 1, u).start()

            plain = [u for u, (j, i) in enumerate(pairs) if j not in RS_XL]
            compute_send(0, 0)
            for u in plain:
                first(u)
            lax.fori_loop(1, 4, compute_send, 0)
            for u in range(count):
                if u not in plain:
                    first(u)
            lax.fori_loop(4, NZ, compute_send, 0)
            for s in range(2, 5):
                for u in range(count):
                    for d in range(2):
                        value = local(2 * s - 3 + d, u)
                        if s > 2 or u % 2 == d:
                            ring(d, s - 1, u).wait_recv()
                            value = value + big_r[spot(d, s - 1, u)].astype(F32)
                        big_s[spot(d, s, u)] = value.astype(BF)
                        ring(d, s, u).start()

            def last(j, i):
                k = j * 2 + i
                n = 24 + 7 * count + pairs.index((j, i)) - 1
                return copy(fin_s.at[k], fin_r.at[k], rs_s, rs_r.at[n], dev(z, y + j, (x + i) % 2, 0))

            for u in list(range(1, count)) + [0]:
                j, i = pairs[u]
                value = local(7, u)
                for d in range(2):
                    ring(d, 4, u).wait_recv()
                    value = value + big_r[spot(d, 4, u)].astype(F32)
                if u:
                    fin_s[j * 2 + i] = value.astype(BF)
                    last(j, i).start()
                else:
                    total[0] = value
            value = total[0]
            for j, i in pairs[1:]:
                last(j, i).wait_recv()
                value = value + fin_r[j * 2 + i].astype(F32)
            finish(value)
            sent(big_s.at[pl.ds(0, 24 + 8 * count - 1)], rs_s, rs_r.at[0])

        @pl.when(c == 1)
        def _():
            def compute(i, carry):
                yy = (y + 2 + i // 2) % NY
                h = i % 2
                half = pl.ds(h * 4, 4)
                unit(yy * 2 + h, trans[half, yy, :, 1], trans_peer[half, yy])
                return carry

            def local(yy, j):
                zz = (z + RS_OFFS[j]) % NZ
                return part[(yy % NY) * 2 + zz // 4, pl.ds((zz % 4) * 2, 2)]

            def ring(d, s, j):
                k = spot(d, s, j)
                span = pl.ds(2 * k, 2)
                return copy(
                    big_s.at[span], big_r.at[span], rs_s, rs_r.at[k], dev(z, y + STEP[d], x, 1)
                )

            def spot(d, s, j):
                return j if s == 1 else 8 + d * 8 + j

            def place(d, s, j):
                return pl.ds(2 * spot(d, s, j), 2)

            lax.fori_loop(0, 2, compute, 0)
            for j in range(8):
                big_s[place(j % 2, 1, j)] = local(y + 2, j).astype(BF)
                ring(j % 2, 1, j).start()
            lax.fori_loop(2, NZ, compute, 0)
            for j in range(8):
                for d in range(2):
                    value = local(y + STEP[d], j)
                    if j % 2 == d:
                        ring(d, 1, j).wait_recv()
                        value = value + big_r[place(d, 1, j)].astype(F32)
                    big_s[place(d, 2, j)] = value.astype(BF)
                    ring(d, 2, j).start()

            def landed(j):
                value = local(y, j)
                for d in range(2):
                    ring(d, 2, j).wait_recv()
                    value = value + big_r[place(d, 2, j)].astype(F32)
                return value

            def ring2(d, s, j):
                k = (s - 1) * 2 + j
                return copy(
                    small_s.at[d, k], small_r.at[d, k], rs_s, rs_r.at[24 + d * 8 + k],
                    dev(z + STEP[d], y, x, 1),
                )

            value = landed(0)
            for j in range(2):
                small_s[j, j] = value[j].astype(BF)
            for j in range(2):
                ring2(j, 1, j).start()
            for s in range(2, 5):
                for d in range(2):
                    value = landed(2 * s - 3 + d)
                    for j in range(2):
                        k = (s - 1) * 2 + j
                        v = value[j]
                        if s > 2 or j == d:
                            ring2(d, s - 1, j).wait_recv()
                            v = v + small_r[d, k - 2].astype(F32)
                        small_s[d, k] = v.astype(BF)
                        ring2(d, s, j).start()
            value = landed(7)
            for j in range(2):
                v = value[j]
                for d in range(2):
                    ring2(d, 4, j).wait_recv()
                    v = v + small_r[d, 6 + j].astype(F32)
                total[j] = v
                fin_s[j] = v.astype(BF)
            last = copy(fin_s.at[1 - x], fin_r.at[1], rs_s, rs_r.at[40], x_next)
            last.start()
            last.wait_recv()
            finish(total[x] + fin_r[1].astype(F32))
            sent(big_s.at[pl.ds(0, 63)], rs_s, rs_r.at[0])

        turned_copy().wait_send()
        sent(delta, dl_s, dl_r)


def shards(token_states, token_ids, master, gain, cand_ids, slab_owner):
    seqs, length, width = token_states.shape[1:]
    tokens = seqs * length
    rows, emb = master.shape[1:]
    vmem = pl.BlockSpec(memory_space=pltpu.VMEM)
    smem = pl.BlockSpec(memory_space=pltpu.SMEM)
    hbm = pl.BlockSpec(memory_space=pl.ANY)
    dma = pltpu.SemaphoreType.DMA
    V = pltpu.VMEM
    out = pl.pallas_call(
        body,
        out_shape=jax.ShapeDtypeStruct((rows, emb), F32),
        in_specs=[hbm, hbm, hbm, vmem, vmem, smem, smem],
        out_specs=vmem,
        scratch_shapes=[
            V((tokens, width), BF),
            V((rows, emb), F32),
            V((1, width), F32),
            V((tokens, width), BF),
            V((NZ, NY, 2, 2, rows, tokens), BF),
            V((NZ, NY, 2, rows, tokens), BF),
            V((NZ, NY, 2, 2, rows, emb), BF),
            V((rows, emb), BF),
            V((tokens, emb), F32),
            V((3, 8, emb // 8), F32),
            V((3, 8, emb // 8), BF),
            V((NZ, NY, 2, 2, 3, 8, emb // 8), BF),
            V((tokens, emb), BF),
            V((tokens, emb), BF),
            V((NZ, 8, rows, emb), F32),
            V((2, rows, emb), F32),
            V((64, rows, emb), BF),
            V((64, rows, emb), BF),
            V((24, rows, emb), BF),
            V((24, rows, emb), BF),
            V((2, 8, rows, emb), BF),
            V((2, 8, rows, emb), BF),
            V((8, rows, emb), BF),
            V((8, rows, emb), BF),
            pltpu.SMEM((24,), jnp.int32),
            dma((3,)),
            dma, dma((64,)),
            dma, dma,
            dma, dma,
            dma, dma,
            dma, dma((2,)),
            dma, dma((8,)),
            dma, dma,
            dma, dma,
            dma, dma((64,)),
        ],
        compiler_params=pltpu.CompilerParams(
            collective_id=0, has_side_effects=True, vmem_limit_bytes=62 * 1024 * 1024
        ),
    )(
        token_states.reshape(tokens, width),
        master[0],
        gain.reshape(1, width),
        token_ids.reshape(seqs, 1, length),
        slab_owner.reshape(3, -1),
        cand_ids,
        slab_owner,
    )
    return out[None]


def solution(mesh):
    placed = (
        P("grp", "fsdp", None, None),
        P("grp", "fsdp", None),
        P("grp", "fsdp", None),
        P(),
        P("fsdp", None),
        P(),
    )
    return jax.shard_map(
        shards, mesh=mesh, in_specs=placed, out_specs=P("grp", "fsdp", None), check_vma=False
    )
```

```python
import jax
import jax.numpy as jnp
from jax import lax
from jax.experimental import pallas as pl
from jax.experimental.pallas import tpu as pltpu
from jax.sharding import PartitionSpec as P

MESH = pl.DeviceIdType.MESH
SHARPNESS = 20.0
NZ, NY = 8, 4
BF, F32 = jnp.bfloat16, jnp.float32
OFFS = (0, -1, 1, -2, 2, -3, 3, 4)
RS_OFFS = (4, 3, -3, 2, -2, 1, -1, 0)
J_ORDER = (0, 1, 3, 2)
AG_XL = (1, 3, 2)
RS_XL = (1, 3, 2)
STEP = (1, -1)
NEAR = (0, 1, -1, 2, -2)
FAR = (3, -3, 4)


def units_of(x_last):
    pairs = []
    for j in J_ORDER:
        pairs.append((j, 0))
        if j not in x_last:
            pairs.append((j, 1))
    return pairs


def body(
    states_hbm, master_hbm, gain_hbm, ids_ref, owner_ref, cand_s, owner_s, out_ref,
    states, master, gain, normed, trans, trans_peer, weight, wrecv, act, stage, stored, slab,
    delta, delta_peer, act_peer, ids_peer, stage_peer, part, total, big_s, big_r, x1_s, x1_r, small_s, small_r, fin_s, fin_r, place_s,
    ld_sem, ag_s, ag_r, fw_s, fw_r, wt_s, wt_r, tp_s, tp_r,
    e1_s, e1_r, e2_s, e2_r, e3_s, e3_r, dl_s, dl_r, ac_s, ac_r, rs_s, rs_r,
):
    g = lax.axis_index("grp")
    f = lax.axis_index("fsdp")
    c = f % 2
    x = (f // 2) % 2
    y = (f // 4) % NY
    z = f // 16
    tokens, width = states.shape
    emb = weight.shape[-1]

    def dev(zz, yy, xx, cc, gg=None):
        index = (((zz % NZ) * NY + yy % NY) * 2 + xx) * 2 + cc
        return (g if gg is None else gg, index)

    def copy(src, dst, ssem, rsem, to):
        return pltpu.make_async_remote_copy(
            src_ref=src, dst_ref=dst, send_sem=ssem, recv_sem=rsem,
            device_id=to, device_id_type=MESH,
        )

    me = (g, f)
    partner = dev(z, y, x, 1 - c)
    x_next = dev(z, y, 1 - x, c)
    trainer = g == 0

    load_master = pltpu.make_async_copy(master_hbm, master, ld_sem.at[0])
    load_gain = pltpu.make_async_copy(gain_hbm, gain, ld_sem.at[1])
    load = pltpu.make_async_copy(states_hbm, states, ld_sem.at[2])
    load_master.start()
    load_gain.start()
    load.start()

    barrier = pltpu.get_barrier_semaphore()
    peers = [dev(z, y + 1, x, c), dev(z, y + 2, x, c), dev(z, y + 3, x, c)]
    peers += [dev(z + 1, y, x, c), dev(z - 1, y, x, c), x_next, partner, (1 - g, f)]
    for peer in peers:
        pl.semaphore_signal(barrier, inc=1, device_id=peer, device_id_type=MESH)
    load_master.wait()
    weight[z, y, x, c] = master[...].astype(BF)
    pl.semaphore_wait(barrier, len(peers))

    def shard(zz, yy, xx, cc):
        return weight.at[zz % NZ, yy % NY, xx % 2, cc]

    def push(ref, ssem, rsem, to):
        copy(ref, ref, ssem, rsem, to).start()

    def got(ref, ssem, rsem):
        copy(ref, ref, ssem, rsem, me).wait_recv()

    def sent(ref, ssem, rsem):
        copy(ref, ref, ssem, rsem, me).wait_send()

    def forward(zz, yy, xx, cc):
        push(shard(zz, yy, xx, cc), fw_s, fw_r, partner)

    own = shard(z, y, x, c)

    def norm_step(i, carry):
        rows = pl.ds(pl.multiple_of(i * 16, 16), 16)
        wide = states[rows, :].astype(F32)
        mean_square = jnp.sum(wide * wide, axis=-1, keepdims=True) * (1.0 / width)
        normed[rows, :] = (wide * lax.rsqrt(mean_square + 1e-05) * gain[...]).astype(BF)
        return carry

    def norm():
        load_gain.wait()
        load.wait()
        lax.fori_loop(0, tokens // 16, norm_step, 0)

    def transpose_step(i, carry):
        columns = pl.ds(pl.multiple_of(i * 512, 512), 512)
        turned = jnp.transpose(normed[:, columns])
        trans[i] = turned.reshape(NY, 2, 2, 32, tokens)
        return carry

    def transpose(lo, hi):
        @pl.when(trainer)
        def _():
            lax.fori_loop(lo, hi, transpose_step, 0)

    def weight_copy():
        return copy(own, wrecv, wt_s, wt_r, (1 - g, f))

    def weight_start():
        @pl.when(trainer)
        def _():
            weight_copy().start()

    @pl.when(c == 0)
    def _():
        units = units_of(AG_XL)

        def ring(zz, u, s, d):
            j, i = units[u]
            push(shard(zz, y + j, x + i, 0), ag_s, ag_r.at[place(d, s, u)], dev(z + STEP[d], y, x, 0))

        def place(d, s, u):
            n = len(units)
            return (s - 1) * 2 * n + d * n + u if s < 4 else 6 * n + u

        base = 7 * len(units)

        def spot(k, j):
            return base + (0 if j == 0 else 1 + k * len(AG_XL) + AG_XL.index(j))

        def cross(k, j):
            push(shard(z + OFFS[k], y + j, x, 0), ag_s, ag_r.at[spot(k, j)], x_next)

        def crossed(k, j):
            got(shard(z + OFFS[k], y + j, x + 1, 0), ag_s, ag_r.at[spot(k, j)])
            forward(z + OFFS[k], y + j, x + 1, 0)

        side = base + 1 + NZ * len(AG_XL)

        for d in range(2):
            ring(z, 0, 1, d)
        cross(0, 0)
        for j in (1, 3, 2):
            push(own, ag_s, ag_r.at[side + j - 1], dev(z, y + j, x, 0))
        forward(z, y, x, 0)
        norm()
        crossed(0, 0)
        for d in range(2):
            ring(z, units.index((0, 1)), 1, d)
        for j in (1, 3, 2):
            got(shard(z, y + j, x, 0), ag_s, ag_r.at[side + (-j) % NY - 1])
            for d in range(2):
                ring(z, units.index((j, 0)), 1, d)
            cross(0, j)
            forward(z, y + j, x, 0)
        transpose(0, 2)

        def serve(k):
            for j in AG_XL:
                crossed(k, j)

        for s in range(2, 5):
            for u, (j, i) in enumerate(units):
                for d in range(2):
                    zz = z - STEP[d] * (s - 1)
                    got(shard(zz, y + j, x + i, 0), ag_s, ag_r.at[place(d, s - 1, u)])
                    if s < 4 or u % 2 == d:
                        ring(zz, u, s, d)
                    if s == 4 and u % 2 == d and j in AG_XL:
                        to = dev(z + STEP[d], y, 1 - x, 0)
                        push(shard(zz, y + j, x, 0), ag_s, ag_r.at[spot(7, j)], to)
                    if j in AG_XL:
                        cross(2 * s - 3 + d, j)
                    forward(zz, y + j, x + i, 0)
            for k in (0,) if s == 2 else (2 * s - 5, 2 * s - 4):
                serve(k)
            transpose(2 * s - 2, 2 * s)
        for u, (j, i) in enumerate(units):
            got(shard(z + 4, y + j, x + i, 0), ag_s, ag_r.at[place(u % 2, 4, u)])
            forward(z + 4, y + j, x + i, 0)
        weight_start()
        for k in (5, 6, 7):
            serve(k)
        sent(big_s.at[pl.ds(0, 7 * len(units) + 1 + NZ * len(AG_XL) + 3)], ag_s, ag_r.at[0])

    @pl.when(c == 1)
    def _():
        def ring(zz, i, s, d):
            push(shard(zz, y, x + i, 1), ag_s, ag_r.at[place(d, s, i)], dev(z + STEP[d], y, x, 1))

        def place(d, s, i):
            return (s - 1) * 4 + d * 2 + i if s < 4 else 12 + i

        def near(d, k, i):
            return 14 + d * 16 + 2 * k + i

        def far(d, k):
            return 46 + d * 8 + k

        def spread(k, i):
            ref = shard(z + OFFS[k], y, x + i, 1)
            for d in range(2):
                push(ref, ag_s, ag_r.at[near(d, k, i)], dev(z, y + STEP[d], x, 1))
            if k == 7:
                push(ref, ag_s, ag_r.at[far(i, k)], dev(z, y + 2, x, 1))
            forward(z + OFFS[k], y, x + i, 1)

        def serve(k):
            for i in range(2):
                for d in range(2):
                    yy = y - STEP[d]
                    ref = shard(z + OFFS[k], yy, x + i, 1)
                    got(ref, ag_s, ag_r.at[near(d, k, i)])
                    if i == d and k < 7:
                        push(ref, ag_s, ag_r.at[far(d, k)], dev(z, y + STEP[d], x, 1))
                    forward(z + OFFS[k], yy, x + i, 1)

        push(own, ag_s, ag_r.at[62], x_next)
        for d in range(2):
            ring(z, 0, 1, d)
        spread(0, 0)
        norm()
        got(shard(z, y, x + 1, 1), ag_s, ag_r.at[62])
        for d in range(2):
            ring(z, 1, 1, d)
        spread(0, 1)
        transpose(0, 1)
        for s in range(2, 5):
            for d in range(2):
                zz = z - STEP[d] * (s - 1)
                for i in range(2):
                    got(shard(zz, y, x + i, 1), ag_s, ag_r.at[place(d, s - 1, i)])
                    if s < 4 or i == d:
                        ring(zz, i, s, d)
                    spread(2 * s - 3 + d, i)
            for k in (0,) if s == 2 else (2 * s - 5, 2 * s - 4):
                serve(k)
            transpose(2 * s - 3, 2 * s - 1)
        for i in range(2):
            got(shard(z + 4, y, x + i, 1), ag_s, ag_r.at[place(i, 4, i)])
            spread(7, i)
        weight_start()
        transpose(7, 8)
        for k in (5, 6, 7):
            serve(k)
        for k in range(NZ):
            for d in range(2):
                got(shard(z + OFFS[k], y + 2, x + d, 1), ag_s, ag_r.at[far(d, k)])
                forward(z + OFFS[k], y + 2, x + d, 1)
        sent(big_s.at[pl.ds(0, 63)], ag_s, ag_r.at[0])

    def turned_copy():
        return copy(trans.at[:, :, :, 1 - c], trans_peer, tp_s, tp_r, partner)

    def act_copies():
        return (
            copy(ids_ref, ids_peer, ac_s.at[0], ac_r.at[0], partner),
            copy(act, act_peer, ac_s.at[1], ac_r.at[1], partner),
        )

    @pl.when(trainer)
    def _():
        turned_copy().start()
        act_copies()[0].start()
        position = (
            lax.broadcasted_iota(jnp.int32, owner_ref.shape, 0) * owner_ref.shape[1]
            + lax.broadcasted_iota(jnp.int32, owner_ref.shape, 1)
        )
        for q in range(3):
            for j in range(8):
                row = cand_s[q, j]
                owner = owner_s[row]
                same = (owner_ref[...] == owner) & (position < row)
                place_s[q * 8 + j] = owner * 3 + jnp.sum(same.astype(jnp.int32))

    got(weight.at[:, :, :, 1 - c], fw_s, fw_r)

    def hidden_step(n, carry):
        columns = pl.ds(pl.multiple_of(n * 256, 256), 256)
        block = weight[:, :, :, :, :, columns].reshape(width, 256)
        hidden = jnp.dot(normed[...], block, preferred_element_type=F32)
        act[:, columns] = jnp.tanh(hidden)
        return carry

    lax.fori_loop(0, emb // 256, hidden_step, 0)

    sent(weight.at[:, :, :, c], fw_s, fw_r)

    @pl.when(trainer)
    def _():
        act_copies()[1].start()

    lanes = emb // 8
    length = tokens // 3
    places = lax.broadcasted_iota(jnp.int32, (length, lanes), 0)
    counts, masks = [], []
    for q in range(3):
        valid = (ids_ref[q] != 0).astype(jnp.int32)
        count = jnp.sum(valid, axis=1, keepdims=True)
        counts.append(count.astype(F32))
        masks.append(places < count)
        for k in range(8):
            block = act[q * length : (q + 1) * length, k * lanes : (k + 1) * lanes]
            sums = jnp.sum(jnp.where(masks[q], block, 0.0), axis=0, keepdims=True)
            stage[q, k : k + 1, :] = sums / counts[q]

    def full_sum(v):
        return jnp.sum(jnp.sum(v, axis=1, keepdims=True), axis=0, keepdims=True)

    pooled, scales, units = [], [], []
    for q in range(3):
        pool = stage[q]
        scale = lax.rsqrt(full_sum(pool * pool) * (1.0 / emb) + 1e-06)
        pooled.append(pool)
        scales.append(scale)
        units.append(pool * scale)

    @pl.when(g == 1)
    def _():
        for q in range(3):
            stored[q] = units[q].astype(BF)
        weight_copy().wait_recv()
        for b in (1, 0):
            for off in (NEAR, FAR)[b]:
                to = dev(z + off, y, x, c, 0)
                copy(stored, slab.at[z, y, x, c], e1_s, e1_r.at[b], to).start()
        out_ref[...] = wrecv[...].astype(F32)
        sent(slab.at[:, 0, 0, 0], e1_s, e1_r.at[0])

    @pl.when(trainer)
    def _():
        sends = [(2, 0), (2, 1), (1, 0), (3, 0), (1, 1), (3, 1), (0, 1)]

        def e2(b, dy, dx):
            to = dev(z, y + dy, (x + dx) % 2, c)
            for off in (NEAR, FAR)[b]:
                push(slab.at[(z + off) % NZ, y, x, c], e2_s, e2_r.at[dy * 2 + dx], to)

        def e3(yy, xx):
            push(slab.at[:, yy % NY, xx, c], e3_s, e3_r, partner)

        for b in range(2):
            got(slab.at[0 : len((NEAR, FAR)[b]), y, x, c], e1_s, e1_r.at[b])
            for dy, dx in sends:
                e2(b, dy, dx)
        e3(y, x)
        for dy, dx in ((0, 1), (1, 0), (3, 0), (1, 1), (3, 1), (2, 0), (2, 1)):
            yy, xx = (y - dy) % NY, (x + dx) % 2
            got(slab.at[:, yy, xx, c], e2_s, e2_r.at[dy * 2 + dx])
            e3(yy, xx)
        got(slab.at[:, :, :, 1 - c], e3_s, e3_r)
        for q in range(3):
            rows, exps = [], []
            for j in range(8):
                p = place_s[q * 8 + j]
                o = p // 3
                row = slab[o // 16, (o // 4) % NY, (o // 2) % 2, o % 2, p - o * 3].astype(F32)
                rows.append(row)
                exps.append(jnp.exp(full_sum(units[q] * row) * (SHARPNESS / emb)))
            norm_sum = exps[0]
            for j in range(1, 8):
                norm_sum = norm_sum + exps[j]
            grad = jnp.zeros_like(rows[0])
            for j in range(8):
                weight_j = exps[j] / norm_sum - (1.0 if j == 0 else 0.0)
                grad = grad + weight_j * rows[j]
            grad = grad * (SHARPNESS / emb)
            inner = full_sum(pooled[q] * grad)
            scale = scales[q]
            stage[q] = scale * grad - pooled[q] * (scale * scale * scale) * inner * (1.0 / emb)
        def fill(q, count, mask, act_ref, stage_ref, delta_ref):
            span = slice(q * length, (q + 1) * length)
            for k in range(8):
                cols = slice(k * lanes, (k + 1) * lanes)
                a = act_ref[span, cols]
                base = jnp.where(mask, 1.0 / count, 0.0) * stage_ref[q, k : k + 1, :]
                delta_ref[span, cols] = (base * (1.0 - a * a)).astype(BF)

        grads = copy(stage, stage_peer, dl_s, dl_r, partner)
        for q in range(3):
            fill(q, counts[q], masks[q], act, stage, delta)
            if q == 0:
                grads.start()
        for pending in act_copies():
            pending.wait()
        grads.wait()
        for q in range(3):
            valid = (ids_peer[q] != 0).astype(jnp.int32)
            count = jnp.sum(valid, axis=1, keepdims=True)
            fill(q, count.astype(F32), places < count, act_peer, stage_peer, delta_peer)
        sent(slab.at[0:7, :, :, 0], e2_s, e2_r.at[0])
        sent(slab.at[:, :, :, c], e3_s, e3_r)
        weight_copy().wait_send()
        turned_copy().wait_recv()

        def unit(u, lhs, lhs_peer):
            value = jnp.dot(lhs.reshape(256, tokens), delta[...], preferred_element_type=F32)
            value = value + jnp.dot(lhs_peer.reshape(256, tokens), delta_peer[...], preferred_element_type=F32)
            part[u] = value.reshape(8, 32, emb)

        def finish(value):
            mean_square = jnp.sum(value * value, axis=1, keepdims=True) * (1.0 / emb)
            out_ref[...] = value * lax.rsqrt(mean_square + 1e-06)

        @pl.when(c == 0)
        def _():
            pairs = [units_of(RS_XL)[q] for q in (1, 2, 3, 4, 0)]
            count = len(pairs)

            def slot(j, i):
                return ((y + j) % NY) * 2 + (x + i) % 2

            def x_first(b, n):
                k = b * 3 + n
                return copy(x1_s.at[k], x1_r.at[k], rs_s, rs_r.at[k], x_next)

            def diagonal(n):
                d = pairs.index((RS_XL[n], 0)) % 2
                to = dev(z + STEP[d], y, 1 - x, 0)
                return copy(x1_s.at[n], x1_r.at[n], rs_s, rs_r.at[n], to)

            def compute(b, carry):
                odd = b % 2
                off = odd * ((7 - b) // 2) - (1 - odd) * ((8 - b) // 2)
                zz = (z + 16 + off) % NZ
                unit(zz, trans[zz, :, :, 0], trans_peer[zz])
                for n, j in enumerate(RS_XL):
                    x1_s[b * 3 + n] = part[zz, slot(j, 1)].astype(BF)
                return carry

            def compute_send(b, carry):
                compute(b, carry)
                for n in range(len(RS_XL)):
                    x_first(b, n).start()
                return carry

            def ring(d, s, u):
                k = spot(d, s, u)
                return copy(big_s.at[k], big_r.at[k], rs_s, rs_r.at[24 + k], dev(z + STEP[d], y, x, 0))

            def spot(d, s, u):
                return u if s == 1 else count + (s - 2) * 2 * count + d * count + u

            def local(b, u):
                j, i = pairs[u]
                value = part[(z + RS_OFFS[b]) % NZ, slot(j, i)]
                if j in RS_XL and b:
                    n = RS_XL.index(j)
                    x_first(b, n).wait_recv()
                    value = value + x1_r[b * 3 + n].astype(F32)
                return value

            def first(u):
                d = u % 2
                big_s[spot(d, 1, u)] = local(0, u).astype(BF)
                ring(d, 1, u).start()

            compute(0, 0)
            for u in range(count):
                first(u)
            for n in range(len(RS_XL)):
                diagonal(n).start()
            lax.fori_loop(1, NZ, compute_send, 0)
            for s in range(2, 5):
                for u in range(count):
                    for d in range(2):
                        value = local(2 * s - 3 + d, u)
                        if s > 2 or u % 2 == d:
                            ring(d, s - 1, u).wait_recv()
                            value = value + big_r[spot(d, s - 1, u)].astype(F32)
                        if s == 2 and u % 2 == d and pairs[u][0] in RS_XL:
                            n = RS_XL.index(pairs[u][0])
                            diagonal(n).wait_recv()
                            value = value + x1_r[n].astype(F32)
                        big_s[spot(d, s, u)] = value.astype(BF)
                        ring(d, s, u).start()

            def last(j, i):
                k = j * 2 + i
                n = 24 + 7 * count + pairs.index((j, i))
                return copy(fin_s.at[k], fin_r.at[k], rs_s, rs_r.at[n], dev(z, y + j, (x + i) % 2, 0))

            for u in range(count):
                j, i = pairs[u]
                value = local(7, u)
                for d in range(2):
                    ring(d, 4, u).wait_recv()
                    value = value + big_r[spot(d, 4, u)].astype(F32)
                if u < count - 1:
                    fin_s[j * 2 + i] = value.astype(BF)
                    last(j, i).start()
                else:
                    total[0] = value
            value = total[0]
            for j, i in pairs[-2::-1]:
                last(j, i).wait_recv()
                value = value + fin_r[j * 2 + i].astype(F32)
            finish(value)
            sent(big_s.at[pl.ds(0, 24 + 8 * count - 1)], rs_s, rs_r.at[0])

        @pl.when(c == 1)
        def _():
            def compute(i, carry):
                yy = (y + 2 + i // 2) % NY
                h = i % 2
                half = pl.ds(h * 4, 4)
                unit(yy * 2 + h, trans[half, yy, :, 1], trans_peer[half, yy])
                return carry

            def local(yy, j):
                zz = (z + RS_OFFS[j]) % NZ
                return part[(yy % NY) * 2 + zz // 4, pl.ds((zz % 4) * 2, 2)]

            def ring(d, s, j):
                k = spot(d, s, j)
                span = pl.ds(2 * k, 2)
                to = dev(z, y + (2 if s == 1 and j == 0 else STEP[d]), x, 1)
                return copy(big_s.at[span], big_r.at[span], rs_s, rs_r.at[k], to)

            def spot(d, s, j):
                return j if s == 1 else 8 + d * 8 + j

            def place(d, s, j):
                return pl.ds(2 * spot(d, s, j), 2)

            lax.fori_loop(0, 2, compute, 0)
            for j in range(8):
                big_s[place(j % 2, 1, j)] = local(y + 2, j).astype(BF)
                ring(j % 2, 1, j).start()
            lax.fori_loop(2, NZ, compute, 0)
            for j in range(8):
                for d in range(2):
                    value = local(y + STEP[d], j)
                    if j and j % 2 == d:
                        ring(d, 1, j).wait_recv()
                        value = value + big_r[place(d, 1, j)].astype(F32)
                    big_s[place(d, 2, j)] = value.astype(BF)
                    ring(d, 2, j).start()

            def landed(j):
                if j == 0:
                    ring(0, 1, 0).wait_recv()
                for d in range(2):
                    ring(d, 2, j).wait_recv()

            def piece(j, i):
                zz = (z + RS_OFFS[j]) % NZ
                side = (x + i) % 2
                value = part[y * 2 + zz // 4, (zz % 4) * 2 + side]
                if j == 0:
                    value = value + big_r[side].astype(F32)
                for d in range(2):
                    value = value + big_r[2 * spot(d, 2, j) + side].astype(F32)
                return value

            def ring2(d, s, i):
                k = (s - 1) * 2 + i
                to = dev(z + STEP[d], y, (x + (i if s == 4 else 0)) % 2, 1)
                return copy(small_s.at[d, k], small_r.at[d, k], rs_s, rs_r.at[24 + d * 8 + k], to)

            landed(0)
            for i in range(2):
                small_s[i, i] = piece(0, i).astype(BF)
                ring2(i, 1, i).start()
            for s in range(2, 5):
                for d in range(2):
                    landed(2 * s - 3 + d)
                    for i in (1, 0):
                        k = (s - 1) * 2 + i
                        value = piece(2 * s - 3 + d, i)
                        if s > 2 or i == d:
                            ring2(d, s - 1, i).wait_recv()
                            value = value + small_r[d, k - 2].astype(F32)
                        small_s[d, k] = value.astype(BF)
                        ring2(d, s, i).start()
            landed(7)
            fin_s[0] = piece(7, 1).astype(BF)
            last = copy(fin_s.at[0], fin_r.at[0], rs_s, rs_r.at[40], x_next)
            last.start()
            value = piece(7, 0)
            for d in range(2):
                for i in range(2):
                    ring2(d, 4, i).wait_recv()
                    value = value + small_r[d, 6 + i].astype(F32)
            last.wait_recv()
            finish(value + fin_r[0].astype(F32))
            sent(big_s.at[pl.ds(0, 63)], rs_s, rs_r.at[0])

        turned_copy().wait_send()


def shards(token_states, token_ids, master, gain, cand_ids, slab_owner):
    seqs, length, width = token_states.shape[1:]
    tokens = seqs * length
    rows, emb = master.shape[1:]
    vmem = pl.BlockSpec(memory_space=pltpu.VMEM)
    smem = pl.BlockSpec(memory_space=pltpu.SMEM)
    hbm = pl.BlockSpec(memory_space=pl.ANY)
    dma = pltpu.SemaphoreType.DMA
    V = pltpu.VMEM
    out = pl.pallas_call(
        body,
        out_shape=jax.ShapeDtypeStruct((rows, emb), F32),
        in_specs=[hbm, hbm, hbm, vmem, vmem, smem, smem],
        out_specs=vmem,
        scratch_shapes=[
            V((tokens, width), BF),
            V((rows, emb), F32),
            V((1, width), F32),
            V((tokens, width), BF),
            V((NZ, NY, 2, 2, rows, tokens), BF),
            V((NZ, NY, 2, rows, tokens), BF),
            V((NZ, NY, 2, 2, rows, emb), BF),
            V((rows, emb), BF),
            V((tokens, emb), F32),
            V((3, 8, emb // 8), F32),
            V((3, 8, emb // 8), BF),
            V((NZ, NY, 2, 2, 3, 8, emb // 8), BF),
            V((tokens, emb), BF),
            V((tokens, emb), BF),
            V((tokens, emb), F32),
            V((seqs, 1, length), jnp.int32),
            V((3, 8, emb // 8), F32),
            V((NZ, 8, rows, emb), F32),
            V((2, rows, emb), F32),
            V((64, rows, emb), BF),
            V((64, rows, emb), BF),
            V((24, rows, emb), BF),
            V((24, rows, emb), BF),
            V((2, 8, rows, emb), BF),
            V((2, 8, rows, emb), BF),
            V((8, rows, emb), BF),
            V((8, rows, emb), BF),
            pltpu.SMEM((24,), jnp.int32),
            dma((3,)),
            dma, dma((64,)),
            dma, dma,
            dma, dma,
            dma, dma,
            dma, dma((2,)),
            dma, dma((8,)),
            dma, dma,
            dma, dma,
            dma((2,)), dma((2,)),
            dma, dma((64,)),
        ],
        compiler_params=pltpu.CompilerParams(
            collective_id=0, has_side_effects=True, vmem_limit_bytes=62 * 1024 * 1024
        ),
    )(
        token_states.reshape(tokens, width),
        master[0],
        gain.reshape(1, width),
        token_ids.reshape(seqs, 1, length),
        slab_owner.reshape(3, -1),
        cand_ids,
        slab_owner,
    )
    return out[None]


def solution(mesh):
    placed = (
        P("grp", "fsdp", None, None),
        P("grp", "fsdp", None),
        P("grp", "fsdp", None),
        P(),
        P("fsdp", None),
        P(),
    )
    return jax.shard_map(
        shards, mesh=mesh, in_specs=placed, out_specs=P("grp", "fsdp", None), check_vma=False
    )
```

```python
import jax
import jax.numpy as jnp
from jax import lax
from jax.experimental import pallas as pl
from jax.experimental.pallas import tpu as pltpu
from jax.sharding import PartitionSpec as P

MESH = pl.DeviceIdType.MESH
SHARPNESS = 20.0
NZ, NY = 8, 4
BF, F32 = jnp.bfloat16, jnp.float32
OFFS = (0, -1, 1, -2, 2, -3, 3, 4)
RS_OFFS = (4, 3, -3, 2, -2, 1, -1, 0)
J_ORDER = (0, 1, 3, 2)
AG_XL = (1, 3, 2)
RS_XL = (1, 3, 2)
STEP = (1, -1)
NEAR = (0, 1, -1, 2, -2)
FAR = (3, -3, 4)


def units_of(x_last):
    pairs = []
    for j in J_ORDER:
        pairs.append((j, 0))
        if j not in x_last:
            pairs.append((j, 1))
    return pairs


def body(
    states_hbm, master_hbm, gain_hbm, ids_ref, owner_ref, cand_s, owner_s, out_ref,
    states, master, gain, normed, trans, trans_peer, weight, wrecv, act, stage, stored, slab,
    deltas, act_peer, ids_peer, stage_peer, part, total, big_s, big_r, x1_s, x1_r, small_s, small_r, fin_s, fin_r, place_s,
    ld_sem, ag_s, ag_r, fw_s, fw_r, wt_s, wt_r, tp_s, tp_r,
    e1_s, e1_r, e2_s, e2_r, e3_s, e3_r, dl_s, dl_r, ac_s, ac_r, rs_s, rs_r,
):
    g = lax.axis_index("grp")
    f = lax.axis_index("fsdp")
    c = f % 2
    x = (f // 2) % 2
    y = (f // 4) % NY
    z = f // 16
    tokens, width = states.shape
    emb = weight.shape[-1]

    def dev(zz, yy, xx, cc, gg=None):
        index = (((zz % NZ) * NY + yy % NY) * 2 + xx) * 2 + cc
        return (g if gg is None else gg, index)

    def copy(src, dst, ssem, rsem, to):
        return pltpu.make_async_remote_copy(
            src_ref=src, dst_ref=dst, send_sem=ssem, recv_sem=rsem,
            device_id=to, device_id_type=MESH,
        )

    me = (g, f)
    partner = dev(z, y, x, 1 - c)
    x_next = dev(z, y, 1 - x, c)
    trainer = g == 0

    load_master = pltpu.make_async_copy(master_hbm, master, ld_sem.at[0])
    load_gain = pltpu.make_async_copy(gain_hbm, gain, ld_sem.at[1])
    load = pltpu.make_async_copy(states_hbm, states, ld_sem.at[2])
    load_master.start()
    load_gain.start()
    load.start()

    barrier = pltpu.get_barrier_semaphore()
    peers = [dev(z, y + 1, x, c), dev(z, y + 2, x, c), dev(z, y + 3, x, c)]
    peers += [dev(z + 1, y, x, c), dev(z - 1, y, x, c), x_next, partner, (1 - g, f)]
    for peer in peers:
        pl.semaphore_signal(barrier, inc=1, device_id=peer, device_id_type=MESH)
    load_master.wait()
    weight[z, y, x, c] = master[...].astype(BF)
    pl.semaphore_wait(barrier, len(peers))

    def shard(zz, yy, xx, cc):
        return weight.at[zz % NZ, yy % NY, xx % 2, cc]

    def push(ref, ssem, rsem, to):
        copy(ref, ref, ssem, rsem, to).start()

    def got(ref, ssem, rsem):
        copy(ref, ref, ssem, rsem, me).wait_recv()

    def sent(ref, ssem, rsem):
        copy(ref, ref, ssem, rsem, me).wait_send()

    def forward(zz, yy, xx, cc):
        push(shard(zz, yy, xx, cc), fw_s, fw_r, partner)

    own = shard(z, y, x, c)

    def norm_step(i, carry):
        rows = pl.ds(pl.multiple_of(i * 16, 16), 16)
        wide = states[rows, :].astype(F32)
        mean_square = jnp.sum(wide * wide, axis=-1, keepdims=True) * (1.0 / width)
        normed[rows, :] = (wide * lax.rsqrt(mean_square + 1e-05) * gain[...]).astype(BF)
        return carry

    def norm():
        load_gain.wait()
        load.wait()
        lax.fori_loop(0, tokens // 16, norm_step, 0)

    def transpose_step(i, carry):
        columns = pl.ds(pl.multiple_of(i * 512, 512), 512)
        turned = jnp.transpose(normed[:, columns])
        trans[i] = turned.reshape(NY, 2, 2, 32, tokens)
        return carry

    def transpose(lo, hi):
        @pl.when(trainer)
        def _():
            lax.fori_loop(lo, hi, transpose_step, 0)

    def weight_copy():
        return copy(own, wrecv, wt_s, wt_r, (1 - g, f))

    def weight_start():
        @pl.when(trainer)
        def _():
            weight_copy().start()

    @pl.when(c == 0)
    def _():
        units = units_of(AG_XL)

        def ring(zz, u, s, d):
            j, i = units[u]
            push(shard(zz, y + j, x + i, 0), ag_s, ag_r.at[place(d, s, u)], dev(z + STEP[d], y, x, 0))

        def place(d, s, u):
            n = len(units)
            return (s - 1) * 2 * n + d * n + u if s < 4 else 6 * n + u

        base = 7 * len(units)

        def spot(k, j):
            return base + (0 if j == 0 else 1 + k * len(AG_XL) + AG_XL.index(j))

        def cross(k, j):
            push(shard(z + OFFS[k], y + j, x, 0), ag_s, ag_r.at[spot(k, j)], x_next)

        def crossed(k, j):
            got(shard(z + OFFS[k], y + j, x + 1, 0), ag_s, ag_r.at[spot(k, j)])
            forward(z + OFFS[k], y + j, x + 1, 0)

        side = base + 1 + NZ * len(AG_XL)

        for d in range(2):
            ring(z, 0, 1, d)
        cross(0, 0)
        for j in (1, 3, 2):
            push(own, ag_s, ag_r.at[side + j - 1], dev(z, y + j, x, 0))
        forward(z, y, x, 0)
        norm()
        crossed(0, 0)
        for d in range(2):
            ring(z, units.index((0, 1)), 1, d)
        for j in (1, 3, 2):
            got(shard(z, y + j, x, 0), ag_s, ag_r.at[side + (-j) % NY - 1])
            for d in range(2):
                ring(z, units.index((j, 0)), 1, d)
            cross(0, j)
            forward(z, y + j, x, 0)
        transpose(0, 2)

        def serve(k):
            for j in AG_XL:
                crossed(k, j)

        for s in range(2, 5):
            for u, (j, i) in enumerate(units):
                for d in range(2):
                    zz = z - STEP[d] * (s - 1)
                    got(shard(zz, y + j, x + i, 0), ag_s, ag_r.at[place(d, s - 1, u)])
                    if s < 4 or u % 2 == d:
                        ring(zz, u, s, d)
                    if s == 4 and u % 2 == d and j in AG_XL:
                        to = dev(z + STEP[d], y, 1 - x, 0)
                        push(shard(zz, y + j, x, 0), ag_s, ag_r.at[spot(7, j)], to)
                    if j in AG_XL:
                        cross(2 * s - 3 + d, j)
                    forward(zz, y + j, x + i, 0)
            for k in (0,) if s == 2 else (2 * s - 5, 2 * s - 4):
                serve(k)
            transpose(2 * s - 2, 2 * s)
        for u, (j, i) in enumerate(units):
            got(shard(z + 4, y + j, x + i, 0), ag_s, ag_r.at[place(u % 2, 4, u)])
            forward(z + 4, y + j, x + i, 0)
        weight_start()
        for k in (5, 6, 7):
            serve(k)
        sent(big_s.at[pl.ds(0, 7 * len(units) + 1 + NZ * len(AG_XL) + 3)], ag_s, ag_r.at[0])

    @pl.when(c == 1)
    def _():
        def ring(zz, i, s, d):
            push(shard(zz, y, x + i, 1), ag_s, ag_r.at[place(d, s, i)], dev(z + STEP[d], y, x, 1))

        def place(d, s, i):
            return (s - 1) * 4 + d * 2 + i if s < 4 else 12 + i

        def near(d, k, i):
            return 14 + d * 16 + 2 * k + i

        def far(d, k):
            return 46 + d * 8 + k

        def spread(k, i):
            ref = shard(z + OFFS[k], y, x + i, 1)
            for d in range(2):
                push(ref, ag_s, ag_r.at[near(d, k, i)], dev(z, y + STEP[d], x, 1))
            if k == 7:
                push(ref, ag_s, ag_r.at[far(i, k)], dev(z, y + 2, x, 1))
            forward(z + OFFS[k], y, x + i, 1)

        def serve(k):
            for i in range(2):
                for d in range(2):
                    yy = y - STEP[d]
                    ref = shard(z + OFFS[k], yy, x + i, 1)
                    got(ref, ag_s, ag_r.at[near(d, k, i)])
                    if i == d and k < 7:
                        push(ref, ag_s, ag_r.at[far(d, k)], dev(z, y + STEP[d], x, 1))
                    forward(z + OFFS[k], yy, x + i, 1)

        push(own, ag_s, ag_r.at[62], x_next)
        for d in range(2):
            ring(z, 0, 1, d)
        spread(0, 0)
        norm()
        got(shard(z, y, x + 1, 1), ag_s, ag_r.at[62])
        for d in range(2):
            ring(z, 1, 1, d)
        spread(0, 1)
        transpose(0, 1)
        for s in range(2, 5):
            for d in range(2):
                zz = z - STEP[d] * (s - 1)
                for i in range(2):
                    got(shard(zz, y, x + i, 1), ag_s, ag_r.at[place(d, s - 1, i)])
                    if s < 4 or i == d:
                        ring(zz, i, s, d)
                    spread(2 * s - 3 + d, i)
            for k in (0,) if s == 2 else (2 * s - 5, 2 * s - 4):
                serve(k)
            transpose(2 * s - 3, 2 * s - 1)
        for i in range(2):
            got(shard(z + 4, y, x + i, 1), ag_s, ag_r.at[place(i, 4, i)])
            spread(7, i)
        weight_start()
        transpose(7, 8)
        for k in (5, 6, 7):
            serve(k)
        for k in range(NZ):
            for d in range(2):
                got(shard(z + OFFS[k], y + 2, x + d, 1), ag_s, ag_r.at[far(d, k)])
                forward(z + OFFS[k], y + 2, x + d, 1)
        sent(big_s.at[pl.ds(0, 63)], ag_s, ag_r.at[0])

    def turned_copy():
        return copy(trans.at[:, :, :, 1 - c], trans_peer, tp_s, tp_r, partner)

    def act_copies():
        return (
            copy(ids_ref, ids_peer, ac_s.at[0], ac_r.at[0], partner),
            copy(act, act_peer, ac_s.at[1], ac_r.at[1], partner),
        )

    @pl.when(trainer)
    def _():
        turned_copy().start()
        act_copies()[0].start()
        position = (
            lax.broadcasted_iota(jnp.int32, owner_ref.shape, 0) * owner_ref.shape[1]
            + lax.broadcasted_iota(jnp.int32, owner_ref.shape, 1)
        )
        for q in range(3):
            for j in range(8):
                row = cand_s[q, j]
                owner = owner_s[row]
                same = (owner_ref[...] == owner) & (position < row)
                place_s[q * 8 + j] = owner * 3 + jnp.sum(same.astype(jnp.int32))

    got(weight.at[:, :, :, 1 - c], fw_s, fw_r)

    def hidden_step(n, carry):
        columns = pl.ds(pl.multiple_of(n * 256, 256), 256)
        block = weight[:, :, :, :, :, columns].reshape(width, 256)
        hidden = jnp.dot(normed[...], block, preferred_element_type=F32)
        act[:, columns] = jnp.tanh(hidden)
        return carry

    lax.fori_loop(0, emb // 256, hidden_step, 0)

    sent(weight.at[:, :, :, c], fw_s, fw_r)

    @pl.when(trainer)
    def _():
        act_copies()[1].start()

    lanes = emb // 8
    length = tokens // 3
    places = lax.broadcasted_iota(jnp.int32, (length, lanes), 0)
    counts, masks = [], []
    for q in range(3):
        valid = (ids_ref[q] != 0).astype(jnp.int32)
        count = jnp.sum(valid, axis=1, keepdims=True)
        counts.append(count.astype(F32))
        masks.append(places < count)
        for k in range(8):
            block = act[q * length : (q + 1) * length, k * lanes : (k + 1) * lanes]
            sums = jnp.sum(jnp.where(masks[q], block, 0.0), axis=0, keepdims=True)
            stage[q, k : k + 1, :] = sums / counts[q]

    def full_sum(v):
        return jnp.sum(jnp.sum(v, axis=1, keepdims=True), axis=0, keepdims=True)

    pooled, scales, units = [], [], []
    for q in range(3):
        pool = stage[q]
        scale = lax.rsqrt(full_sum(pool * pool) * (1.0 / emb) + 1e-06)
        pooled.append(pool)
        scales.append(scale)
        units.append(pool * scale)

    @pl.when(g == 1)
    def _():
        for q in range(3):
            stored[q] = units[q].astype(BF)
        weight_copy().wait_recv()
        for b in (1, 0):
            for off in (NEAR, FAR)[b]:
                to = dev(z + off, y, x, c, 0)
                copy(stored, slab.at[z, y, x, c], e1_s, e1_r.at[b], to).start()
        out_ref[...] = wrecv[...].astype(F32)
        sent(slab.at[:, 0, 0, 0], e1_s, e1_r.at[0])

    @pl.when(trainer)
    def _():
        sends = [(2, 0), (2, 1), (1, 0), (3, 0), (1, 1), (3, 1), (0, 1)]

        def e2(b, dy, dx):
            to = dev(z, y + dy, (x + dx) % 2, c)
            for off in (NEAR, FAR)[b]:
                push(slab.at[(z + off) % NZ, y, x, c], e2_s, e2_r.at[dy * 2 + dx], to)

        def e3(yy, xx):
            push(slab.at[:, yy % NY, xx, c], e3_s, e3_r, partner)

        for b in range(2):
            got(slab.at[0 : len((NEAR, FAR)[b]), y, x, c], e1_s, e1_r.at[b])
            for dy, dx in sends:
                e2(b, dy, dx)
        e3(y, x)
        for dy, dx in ((0, 1), (1, 0), (3, 0), (1, 1), (3, 1), (2, 0), (2, 1)):
            yy, xx = (y - dy) % NY, (x + dx) % 2
            got(slab.at[:, yy, xx, c], e2_s, e2_r.at[dy * 2 + dx])
            e3(yy, xx)
        got(slab.at[:, :, :, 1 - c], e3_s, e3_r)
        for q in range(3):
            rows, exps = [], []
            for j in range(8):
                p = place_s[q * 8 + j]
                o = p // 3
                row = slab[o // 16, (o // 4) % NY, (o // 2) % 2, o % 2, p - o * 3].astype(F32)
                rows.append(row)
                exps.append(jnp.exp(full_sum(units[q] * row) * (SHARPNESS / emb)))
            norm_sum = exps[0]
            for j in range(1, 8):
                norm_sum = norm_sum + exps[j]
            grad = jnp.zeros_like(rows[0])
            for j in range(8):
                weight_j = exps[j] / norm_sum - (1.0 if j == 0 else 0.0)
                grad = grad + weight_j * rows[j]
            grad = grad * (SHARPNESS / emb)
            inner = full_sum(pooled[q] * grad)
            scale = scales[q]
            stage[q] = scale * grad - pooled[q] * (scale * scale * scale) * inner * (1.0 / emb)
        def fill(q, count, mask, act_ref, stage_ref, base_row):
            span = slice(q * length, (q + 1) * length)
            for k in range(8):
                cols = slice(k * lanes, (k + 1) * lanes)
                a = act_ref[span, cols]
                base = jnp.where(mask, 1.0 / count, 0.0) * stage_ref[q, k : k + 1, :]
                rows = slice(base_row + q * length, base_row + (q + 1) * length)
                deltas[rows, cols] = (base * (1.0 - a * a)).astype(BF)

        grads = copy(stage, stage_peer, dl_s, dl_r, partner)
        for q in range(3):
            fill(q, counts[q], masks[q], act, stage, 0)
            if q == 0:
                grads.start()
        for pending in act_copies():
            pending.wait()
        grads.wait()
        for q in range(3):
            valid = (ids_peer[q] != 0).astype(jnp.int32)
            count = jnp.sum(valid, axis=1, keepdims=True)
            fill(q, count.astype(F32), places < count, act_peer, stage_peer, tokens)
        sent(slab.at[0:7, :, :, 0], e2_s, e2_r.at[0])
        sent(slab.at[:, :, :, c], e3_s, e3_r)
        weight_copy().wait_send()
        turned_copy().wait_recv()

        def unit(u, lhs, lhs_peer):
            both = jnp.concatenate([lhs.reshape(256, tokens), lhs_peer.reshape(256, tokens)], axis=1)
            value = jnp.dot(both, deltas[...], preferred_element_type=F32)
            part[u] = value.reshape(8, 32, emb)

        def finish(value):
            mean_square = jnp.sum(value * value, axis=1, keepdims=True) * (1.0 / emb)
            out_ref[...] = value * lax.rsqrt(mean_square + 1e-06)

        @pl.when(c == 0)
        def _():
            pairs = [units_of(RS_XL)[q] for q in (1, 2, 3, 4, 0)]
            count = len(pairs)

            def slot(j, i):
                return ((y + j) % NY) * 2 + (x + i) % 2

            def x_first(b, n):
                k = b * 3 + n
                return copy(x1_s.at[k], x1_r.at[k], rs_s, rs_r.at[k], x_next)

            def diagonal(n):
                d = pairs.index((RS_XL[n], 0)) % 2
                to = dev(z + STEP[d], y, 1 - x, 0)
                return copy(x1_s.at[n], x1_r.at[n], rs_s, rs_r.at[n], to)

            def compute(b, carry):
                odd = b % 2
                off = odd * ((7 - b) // 2) - (1 - odd) * ((8 - b) // 2)
                zz = (z + 16 + off) % NZ
                unit(zz, trans[zz, :, :, 0], trans_peer[zz])
                for n, j in enumerate(RS_XL):
                    x1_s[b * 3 + n] = part[zz, slot(j, 1)].astype(BF)
                return carry

            def compute_send(b, carry):
                compute(b, carry)
                for n in range(len(RS_XL)):
                    x_first(b, n).start()
                return carry

            def ring(d, s, u):
                k = spot(d, s, u)
                return copy(big_s.at[k], big_r.at[k], rs_s, rs_r.at[24 + k], dev(z + STEP[d], y, x, 0))

            def spot(d, s, u):
                return u if s == 1 else count + (s - 2) * 2 * count + d * count + u

            def local(b, u):
                j, i = pairs[u]
                value = part[(z + RS_OFFS[b]) % NZ, slot(j, i)]
                if j in RS_XL and b:
                    n = RS_XL.index(j)
                    x_first(b, n).wait_recv()
                    value = value + x1_r[b * 3 + n].astype(F32)
                return value

            def first(u):
                d = u % 2
                big_s[spot(d, 1, u)] = local(0, u).astype(BF)
                ring(d, 1, u).start()

            compute(0, 0)
            for u in range(count):
                first(u)
            for n in range(len(RS_XL)):
                diagonal(n).start()
            lax.fori_loop(1, NZ, compute_send, 0)
            for s in range(2, 5):
                for u in range(count):
                    for d in range(2):
                        value = local(2 * s - 3 + d, u)
                        if s > 2 or u % 2 == d:
                            ring(d, s - 1, u).wait_recv()
                            value = value + big_r[spot(d, s - 1, u)].astype(F32)
                        if s == 2 and u % 2 == d and pairs[u][0] in RS_XL:
                            n = RS_XL.index(pairs[u][0])
                            diagonal(n).wait_recv()
                            value = value + x1_r[n].astype(F32)
                        big_s[spot(d, s, u)] = value.astype(BF)
                        ring(d, s, u).start()

            def last(j, i):
                k = j * 2 + i
                n = 24 + 7 * count + pairs.index((j, i))
                return copy(fin_s.at[k], fin_r.at[k], rs_s, rs_r.at[n], dev(z, y + j, (x + i) % 2, 0))

            for u in range(count):
                j, i = pairs[u]
                value = local(7, u)
                for d in range(2):
                    ring(d, 4, u).wait_recv()
                    value = value + big_r[spot(d, 4, u)].astype(F32)
                if u < count - 1:
                    fin_s[j * 2 + i] = value.astype(BF)
                    last(j, i).start()
                else:
                    total[0] = value
            value = total[0]
            for j, i in pairs[-2::-1]:
                last(j, i).wait_recv()
                value = value + fin_r[j * 2 + i].astype(F32)
            finish(value)
            sent(big_s.at[pl.ds(0, 24 + 8 * count - 1)], rs_s, rs_r.at[0])

        @pl.when(c == 1)
        def _():
            def compute(off):
                yy = (y + off) % NY

                def one(h, carry):
                    half = pl.ds(h * 4, 4)
                    unit(yy * 2 + h, trans[half, yy, :, 1], trans_peer[half, yy])
                    return carry

                lax.fori_loop(0, 2, one, 0)

            def local(yy, j):
                zz = (z + RS_OFFS[j]) % NZ
                return part[(yy % NY) * 2 + zz // 4, pl.ds((zz % 4) * 2, 2)]

            def ring(d, s, j):
                k = spot(d, s, j)
                span = pl.ds(2 * k, 2)
                to = dev(z, y + (2 if s == 1 and j == 0 else STEP[d]), x, 1)
                return copy(big_s.at[span], big_r.at[span], rs_s, rs_r.at[k], to)

            def spot(d, s, j):
                return j if s == 1 else 8 + d * 8 + j

            def place(d, s, j):
                return pl.ds(2 * spot(d, s, j), 2)

            def opposite(j):
                big_s[place(j % 2, 1, j)] = local(y + 2, j).astype(BF)
                ring(j % 2, 1, j).start()

            def nearest(j):
                for d in range(2):
                    value = local(y + STEP[d], j)
                    if j and j % 2 == d:
                        ring(d, 1, j).wait_recv()
                        value = value + big_r[place(d, 1, j)].astype(F32)
                    big_s[place(d, 2, j)] = value.astype(BF)
                    ring(d, 2, j).start()

            compute(2)
            for j in range(4):
                opposite(j)
            compute(3)
            compute(1)
            nearest(0)
            for j in range(4, 8):
                opposite(j)
            compute(0)
            for j in range(1, 4):
                nearest(j)

            def landed(j):
                if j == 0:
                    ring(0, 1, 0).wait_recv()
                for d in range(2):
                    ring(d, 2, j).wait_recv()

            def piece(j, i):
                zz = (z + RS_OFFS[j]) % NZ
                side = (x + i) % 2
                value = part[y * 2 + zz // 4, (zz % 4) * 2 + side]
                if j == 0:
                    value = value + big_r[side].astype(F32)
                for d in range(2):
                    value = value + big_r[2 * spot(d, 2, j) + side].astype(F32)
                return value

            def ring2(d, s, i):
                k = (s - 1) * 2 + i
                to = dev(z + STEP[d], y, (x + (i if s == 4 else 0)) % 2, 1)
                return copy(small_s.at[d, k], small_r.at[d, k], rs_s, rs_r.at[24 + d * 8 + k], to)

            landed(0)
            for i in range(2):
                small_s[i, i] = piece(0, i).astype(BF)
                ring2(i, 1, i).start()
            for j in range(4, 8):
                nearest(j)
            for s in range(2, 5):
                for d in range(2):
                    landed(2 * s - 3 + d)
                    for i in (1, 0):
                        k = (s - 1) * 2 + i
                        value = piece(2 * s - 3 + d, i)
                        if s > 2 or i == d:
                            ring2(d, s - 1, i).wait_recv()
                            value = value + small_r[d, k - 2].astype(F32)
                        small_s[d, k] = value.astype(BF)
                        ring2(d, s, i).start()
            landed(7)
            fin_s[0] = piece(7, 1).astype(BF)
            last = copy(fin_s.at[0], fin_r.at[0], rs_s, rs_r.at[40], x_next)
            last.start()
            value = piece(7, 0)
            for d in range(2):
                for i in range(2):
                    ring2(d, 4, i).wait_recv()
                    value = value + small_r[d, 6 + i].astype(F32)
            last.wait_recv()
            finish(value + fin_r[0].astype(F32))
            sent(big_s.at[pl.ds(0, 63)], rs_s, rs_r.at[0])

        turned_copy().wait_send()


def shards(token_states, token_ids, master, gain, cand_ids, slab_owner):
    seqs, length, width = token_states.shape[1:]
    tokens = seqs * length
    rows, emb = master.shape[1:]
    vmem = pl.BlockSpec(memory_space=pltpu.VMEM)
    smem = pl.BlockSpec(memory_space=pltpu.SMEM)
    hbm = pl.BlockSpec(memory_space=pl.ANY)
    dma = pltpu.SemaphoreType.DMA
    V = pltpu.VMEM
    out = pl.pallas_call(
        body,
        out_shape=jax.ShapeDtypeStruct((rows, emb), F32),
        in_specs=[hbm, hbm, hbm, vmem, vmem, smem, smem],
        out_specs=vmem,
        scratch_shapes=[
            V((tokens, width), BF),
            V((rows, emb), F32),
            V((1, width), F32),
            V((tokens, width), BF),
            V((NZ, NY, 2, 2, rows, tokens), BF),
            V((NZ, NY, 2, rows, tokens), BF),
            V((NZ, NY, 2, 2, rows, emb), BF),
            V((rows, emb), BF),
            V((tokens, emb), F32),
            V((3, 8, emb // 8), F32),
            V((3, 8, emb // 8), BF),
            V((NZ, NY, 2, 2, 3, 8, emb // 8), BF),
            V((2 * tokens, emb), BF),
            V((tokens, emb), F32),
            V((seqs, 1, length), jnp.int32),
            V((3, 8, emb // 8), F32),
            V((NZ, 8, rows, emb), F32),
            V((2, rows, emb), F32),
            V((64, rows, emb), BF),
            V((64, rows, emb), BF),
            V((24, rows, emb), BF),
            V((24, rows, emb), BF),
            V((2, 8, rows, emb), BF),
            V((2, 8, rows, emb), BF),
            V((8, rows, emb), BF),
            V((8, rows, emb), BF),
            pltpu.SMEM((24,), jnp.int32),
            dma((3,)),
            dma, dma((64,)),
            dma, dma,
            dma, dma,
            dma, dma,
            dma, dma((2,)),
            dma, dma((8,)),
            dma, dma,
            dma, dma,
            dma((2,)), dma((2,)),
            dma, dma((64,)),
        ],
        compiler_params=pltpu.CompilerParams(
            collective_id=0, has_side_effects=True, vmem_limit_bytes=62 * 1024 * 1024
        ),
    )(
        token_states.reshape(tokens, width),
        master[0],
        gain.reshape(1, width),
        token_ids.reshape(seqs, 1, length),
        slab_owner.reshape(3, -1),
        cand_ids,
        slab_owner,
    )
    return out[None]


def solution(mesh):
    placed = (
        P("grp", "fsdp", None, None),
        P("grp", "fsdp", None),
        P("grp", "fsdp", None),
        P(),
        P("fsdp", None),
        P(),
    )
    return jax.shard_map(
        shards, mesh=mesh, in_specs=placed, out_specs=P("grp", "fsdp", None), check_vma=False
    )
```

```python
import jax
import jax.numpy as jnp
from jax import lax
from jax.experimental import pallas as pl
from jax.experimental.pallas import tpu as pltpu
from jax.sharding import PartitionSpec as P

MESH = pl.DeviceIdType.MESH
SHARPNESS = 20.0
NZ, NY = 8, 4
BF, F32 = jnp.bfloat16, jnp.float32
OFFS = (0, -1, 1, -2, 2, -3, 3, 4)
RS_OFFS = (4, 3, -3, 2, -2, 1, -1, 0)
J_ORDER = (0, 1, 3, 2)
AG_XL = (1, 3, 2)
RS_XL = (1, 3, 2)
STEP = (1, -1)
BATCHES = ((0, 1, -1), (2, -2), (3, -3, 4))


def units_of(x_last):
    pairs = []
    for j in J_ORDER:
        pairs.append((j, 0))
        if j not in x_last:
            pairs.append((j, 1))
    return pairs


def body(
    states_hbm, master_hbm, gain_hbm, ids_ref, owner_ref, cand_s, owner_s, out_ref,
    states, master, gain, normed, trans, trans_peer, weight, wrecv, act, stage, stored, slab,
    delta, delta_peer, act_peer, ids_peer, stage_peer, part, total, big_s, big_r, x1_s, x1_r, small_s, small_r, fin_s, fin_r, place_s,
    ld_sem, ag_s, ag_r, fw_s, fw_r, wt_s, wt_r, tp_s, tp_r,
    e1_s, e1_r, e2_s, e2_r, e3_s, e3_r, dl_s, dl_r, ac_s, ac_r, rs_s, rs_r,
):
    g = lax.axis_index("grp")
    f = lax.axis_index("fsdp")
    c = f % 2
    x = (f // 2) % 2
    y = (f // 4) % NY
    z = f // 16
    tokens, width = states.shape
    emb = weight.shape[-1]

    def dev(zz, yy, xx, cc, gg=None):
        index = (((zz % NZ) * NY + yy % NY) * 2 + xx) * 2 + cc
        return (g if gg is None else gg, index)

    def copy(src, dst, ssem, rsem, to):
        return pltpu.make_async_remote_copy(
            src_ref=src, dst_ref=dst, send_sem=ssem, recv_sem=rsem,
            device_id=to, device_id_type=MESH,
        )

    me = (g, f)
    partner = dev(z, y, x, 1 - c)
    x_next = dev(z, y, 1 - x, c)
    trainer = g == 0

    load_master = pltpu.make_async_copy(master_hbm, master, ld_sem.at[0])
    load_gain = pltpu.make_async_copy(gain_hbm, gain, ld_sem.at[1])
    load = pltpu.make_async_copy(states_hbm, states, ld_sem.at[2])
    load_master.start()
    load_gain.start()
    load.start()

    barrier = pltpu.get_barrier_semaphore()
    peers = [dev(z, y + 1, x, c), dev(z, y + 2, x, c), dev(z, y + 3, x, c)]
    peers += [dev(z + 1, y, x, c), dev(z - 1, y, x, c), x_next, partner, (1 - g, f)]
    for peer in peers:
        pl.semaphore_signal(barrier, inc=1, device_id=peer, device_id_type=MESH)
    load_master.wait()
    weight[z, y, x, c] = master[...].astype(BF)
    pl.semaphore_wait(barrier, len(peers))

    def shard(zz, yy, xx, cc):
        return weight.at[zz % NZ, yy % NY, xx % 2, cc]

    def push(ref, ssem, rsem, to):
        copy(ref, ref, ssem, rsem, to).start()

    def got(ref, ssem, rsem):
        copy(ref, ref, ssem, rsem, me).wait_recv()

    def sent(ref, ssem, rsem):
        copy(ref, ref, ssem, rsem, me).wait_send()

    def forward(zz, yy, xx, cc):
        push(shard(zz, yy, xx, cc), fw_s, fw_r, partner)

    own = shard(z, y, x, c)

    def norm_step(i, carry):
        rows = pl.ds(pl.multiple_of(i * 16, 16), 16)
        wide = states[rows, :].astype(F32)
        mean_square = jnp.sum(wide * wide, axis=-1, keepdims=True) * (1.0 / width)
        normed[rows, :] = (wide * lax.rsqrt(mean_square + 1e-05) * gain[...]).astype(BF)
        return carry

    def norm():
        load_gain.wait()
        load.wait()
        lax.fori_loop(0, tokens // 16, norm_step, 0)

    def transpose_step(i, carry):
        columns = pl.ds(pl.multiple_of(i * 512, 512), 512)
        turned = jnp.transpose(normed[:, columns])
        trans[i] = turned.reshape(NY, 2, 2, 32, tokens)
        return carry

    def transpose(lo, hi):
        @pl.when(trainer)
        def _():
            lax.fori_loop(lo, hi, transpose_step, 0)

    def weight_copy():
        return copy(own, wrecv, wt_s, wt_r, (1 - g, f))

    def weight_start():
        @pl.when(trainer)
        def _():
            weight_copy().start()

    @pl.when(c == 0)
    def _():
        units = units_of(AG_XL)

        def ring(zz, u, s, d):
            j, i = units[u]
            push(shard(zz, y + j, x + i, 0), ag_s, ag_r.at[place(d, s, u)], dev(z + STEP[d], y, x, 0))

        def place(d, s, u):
            n = len(units)
            return (s - 1) * 2 * n + d * n + u if s < 4 else 6 * n + u

        base = 7 * len(units)

        def spot(k, j):
            return base + (0 if j == 0 else 1 + k * len(AG_XL) + AG_XL.index(j))

        def cross(k, j):
            push(shard(z + OFFS[k], y + j, x, 0), ag_s, ag_r.at[spot(k, j)], x_next)

        def crossed(k, j):
            got(shard(z + OFFS[k], y + j, x + 1, 0), ag_s, ag_r.at[spot(k, j)])
            forward(z + OFFS[k], y + j, x + 1, 0)

        side = base + 1 + NZ * len(AG_XL)

        for d in range(2):
            ring(z, 0, 1, d)
        cross(0, 0)
        for j in (1, 3, 2):
            push(own, ag_s, ag_r.at[side + j - 1], dev(z, y + j, x, 0))
        forward(z, y, x, 0)
        norm()
        crossed(0, 0)
        for d in range(2):
            ring(z, units.index((0, 1)), 1, d)
        for j in (1, 3, 2):
            got(shard(z, y + j, x, 0), ag_s, ag_r.at[side + (-j) % NY - 1])
            for d in range(2):
                ring(z, units.index((j, 0)), 1, d)
            cross(0, j)
            forward(z, y + j, x, 0)
        transpose(0, 2)

        def serve(k):
            for j in AG_XL:
                crossed(k, j)

        for s in range(2, 5):
            for u, (j, i) in enumerate(units):
                for d in range(2):
                    zz = z - STEP[d] * (s - 1)
                    got(shard(zz, y + j, x + i, 0), ag_s, ag_r.at[place(d, s - 1, u)])
                    if s < 4 or u % 2 == d:
                        ring(zz, u, s, d)
                    if s == 4 and u % 2 == d and j in AG_XL:
                        to = dev(z + STEP[d], y, 1 - x, 0)
                        push(shard(zz, y + j, x, 0), ag_s, ag_r.at[spot(7, j)], to)
                    if j in AG_XL:
                        cross(2 * s - 3 + d, j)
                    forward(zz, y + j, x + i, 0)
            for k in (0,) if s == 2 else (2 * s - 5, 2 * s - 4):
                serve(k)
            transpose(2 * s - 2, 2 * s)
        for u, (j, i) in enumerate(units):
            got(shard(z + 4, y + j, x + i, 0), ag_s, ag_r.at[place(u % 2, 4, u)])
            forward(z + 4, y + j, x + i, 0)
        weight_start()
        for k in (5, 6, 7):
            serve(k)
        sent(big_s.at[pl.ds(0, 7 * len(units) + 1 + NZ * len(AG_XL) + 3)], ag_s, ag_r.at[0])

    @pl.when(c == 1)
    def _():
        def ring(zz, i, s, d):
            push(shard(zz, y, x + i, 1), ag_s, ag_r.at[place(d, s, i)], dev(z + STEP[d], y, x, 1))

        def place(d, s, i):
            return (s - 1) * 4 + d * 2 + i if s < 4 else 12 + i

        def near(d, k, i):
            return 14 + d * 16 + 2 * k + i

        def far(d, k):
            return 46 + d * 8 + k

        def spread(k, i):
            ref = shard(z + OFFS[k], y, x + i, 1)
            for d in range(2):
                push(ref, ag_s, ag_r.at[near(d, k, i)], dev(z, y + STEP[d], x, 1))
            if k == 7:
                push(ref, ag_s, ag_r.at[far(i, k)], dev(z, y + 2, x, 1))
            forward(z + OFFS[k], y, x + i, 1)

        def serve(k):
            for i in range(2):
                for d in range(2):
                    yy = y - STEP[d]
                    ref = shard(z + OFFS[k], yy, x + i, 1)
                    got(ref, ag_s, ag_r.at[near(d, k, i)])
                    if i == d and k < 7:
                        push(ref, ag_s, ag_r.at[far(d, k)], dev(z, y + STEP[d], x, 1))
                    forward(z + OFFS[k], yy, x + i, 1)

        push(own, ag_s, ag_r.at[62], x_next)
        for d in range(2):
            ring(z, 0, 1, d)
        spread(0, 0)
        norm()
        got(shard(z, y, x + 1, 1), ag_s, ag_r.at[62])
        for d in range(2):
            ring(z, 1, 1, d)
        spread(0, 1)
        transpose(0, 1)
        for s in range(2, 5):
            for d in range(2):
                zz = z - STEP[d] * (s - 1)
                for i in range(2):
                    got(shard(zz, y, x + i, 1), ag_s, ag_r.at[place(d, s - 1, i)])
                    if s < 4 or i == d:
                        ring(zz, i, s, d)
                    spread(2 * s - 3 + d, i)
            for k in (0,) if s == 2 else (2 * s - 5, 2 * s - 4):
                serve(k)
            transpose(2 * s - 3, 2 * s - 1)
        for i in range(2):
            got(shard(z + 4, y, x + i, 1), ag_s, ag_r.at[place(i, 4, i)])
            spread(7, i)
        weight_start()
        transpose(7, 8)
        for k in (5, 6, 7):
            serve(k)
        for k in range(NZ):
            for d in range(2):
                got(shard(z + OFFS[k], y + 2, x + d, 1), ag_s, ag_r.at[far(d, k)])
                forward(z + OFFS[k], y + 2, x + d, 1)
        sent(big_s.at[pl.ds(0, 63)], ag_s, ag_r.at[0])

    def turned_copy():
        return copy(trans.at[:, :, :, 1 - c], trans_peer, tp_s, tp_r, partner)

    def act_copies():
        return (
            copy(ids_ref, ids_peer, ac_s.at[0], ac_r.at[0], partner),
            copy(act, act_peer, ac_s.at[1], ac_r.at[1], partner),
        )

    @pl.when(trainer)
    def _():
        turned_copy().start()
        act_copies()[0].start()
        position = (
            lax.broadcasted_iota(jnp.int32, owner_ref.shape, 0) * owner_ref.shape[1]
            + lax.broadcasted_iota(jnp.int32, owner_ref.shape, 1)
        )
        for q in range(3):
            for j in range(8):
                row = cand_s[q, j]
                owner = owner_s[row]
                same = (owner_ref[...] == owner) & (position < row)
                place_s[q * 8 + j] = owner * 3 + jnp.sum(same.astype(jnp.int32))

    got(weight.at[:, :, :, 1 - c], fw_s, fw_r)

    def hidden_step(n, carry):
        columns = pl.ds(pl.multiple_of(n * 256, 256), 256)
        block = weight[:, :, :, :, :, columns].reshape(width, 256)
        hidden = jnp.dot(normed[...], block, preferred_element_type=F32)
        act[:, columns] = jnp.tanh(hidden)
        return carry

    lax.fori_loop(0, emb // 256, hidden_step, 0)

    sent(weight.at[:, :, :, c], fw_s, fw_r)

    @pl.when(trainer)
    def _():
        act_copies()[1].start()

    lanes = emb // 8
    length = tokens // 3
    places = lax.broadcasted_iota(jnp.int32, (length, lanes), 0)
    counts, masks = [], []
    for q in range(3):
        valid = (ids_ref[q] != 0).astype(jnp.int32)
        count = jnp.sum(valid, axis=1, keepdims=True)
        counts.append(count.astype(F32))
        masks.append(places < count)
        for k in range(8):
            block = act[q * length : (q + 1) * length, k * lanes : (k + 1) * lanes]
            sums = jnp.sum(jnp.where(masks[q], block, 0.0), axis=0, keepdims=True)
            stage[q, k : k + 1, :] = sums / counts[q]

    def full_sum(v):
        return jnp.sum(jnp.sum(v, axis=1, keepdims=True), axis=0, keepdims=True)

    pooled, scales, units = [], [], []
    for q in range(3):
        pool = stage[q]
        scale = lax.rsqrt(full_sum(pool * pool) * (1.0 / emb) + 1e-06)
        pooled.append(pool)
        scales.append(scale)
        units.append(pool * scale)

    @pl.when(g == 1)
    def _():
        for q in range(3):
            stored[q] = units[q].astype(BF)
        weight_copy().wait_recv()
        for b in (2, 1, 0):
            for off in BATCHES[b]:
                to = dev(z + off, y, x, c, 0)
                copy(stored, slab.at[z, y, x, c], e1_s, e1_r.at[b], to).start()
        out_ref[...] = wrecv[...].astype(F32)
        sent(slab.at[:, 0, 0, 0], e1_s, e1_r.at[0])

    @pl.when(trainer)
    def _():
        sends = [(2, 0), (2, 1), (1, 0), (3, 0), (1, 1), (3, 1), (0, 1)]

        def e2(b, dy, dx):
            to = dev(z, y + dy, (x + dx) % 2, c)
            for off in BATCHES[b]:
                push(slab.at[(z + off) % NZ, y, x, c], e2_s, e2_r.at[dy * 2 + dx], to)

        def e3(yy, xx):
            push(slab.at[:, yy % NY, xx, c], e3_s, e3_r, partner)

        for b in range(3):
            got(slab.at[0 : len(BATCHES[b]), y, x, c], e1_s, e1_r.at[b])
            for dy, dx in sends:
                e2(b, dy, dx)
        e3(y, x)
        for dy, dx in ((0, 1), (1, 0), (3, 0), (1, 1), (3, 1), (2, 0), (2, 1)):
            yy, xx = (y - dy) % NY, (x + dx) % 2
            got(slab.at[:, yy, xx, c], e2_s, e2_r.at[dy * 2 + dx])
            e3(yy, xx)
        got(slab.at[:, :, :, 1 - c], e3_s, e3_r)
        for q in range(3):
            rows, exps = [], []
            for j in range(8):
                p = place_s[q * 8 + j]
                o = p // 3
                row = slab[o // 16, (o // 4) % NY, (o // 2) % 2, o % 2, p - o * 3].astype(F32)
                rows.append(row)
                exps.append(jnp.exp(full_sum(units[q] * row) * (SHARPNESS / emb)))
            norm_sum = exps[0]
            for j in range(1, 8):
                norm_sum = norm_sum + exps[j]
            grad = jnp.zeros_like(rows[0])
            for j in range(8):
                weight_j = exps[j] / norm_sum - (1.0 if j == 0 else 0.0)
                grad = grad + weight_j * rows[j]
            grad = grad * (SHARPNESS / emb)
            inner = full_sum(pooled[q] * grad)
            scale = scales[q]
            stage[q] = scale * grad - pooled[q] * (scale * scale * scale) * inner * (1.0 / emb)
        def fill(q, count, mask, act_ref, stage_ref, delta_ref):
            span = slice(q * length, (q + 1) * length)
            for k in range(8):
                cols = slice(k * lanes, (k + 1) * lanes)
                a = act_ref[span, cols]
                base = jnp.where(mask, 1.0 / count, 0.0) * stage_ref[q, k : k + 1, :]
                delta_ref[span, cols] = (base * (1.0 - a * a)).astype(BF)

        grads = copy(stage, stage_peer, dl_s, dl_r, partner)
        for q in range(3):
            fill(q, counts[q], masks[q], act, stage, delta)
            if q == 0:
                grads.start()
        for pending in act_copies():
            pending.wait()
        grads.wait()
        for q in range(3):
            valid = (ids_peer[q] != 0).astype(jnp.int32)
            count = jnp.sum(valid, axis=1, keepdims=True)
            fill(q, count.astype(F32), places < count, act_peer, stage_peer, delta_peer)
        sent(slab.at[0:7, :, :, 0], e2_s, e2_r.at[0])
        sent(slab.at[:, :, :, c], e3_s, e3_r)
        weight_copy().wait_send()
        turned_copy().wait_recv()

        def unit(u, lhs, lhs_peer):
            value = jnp.dot(lhs.reshape(256, tokens), delta[...], preferred_element_type=F32)
            value = value + jnp.dot(lhs_peer.reshape(256, tokens), delta_peer[...], preferred_element_type=F32)
            part[u] = value.reshape(8, 32, emb)

        def finish(value):
            mean_square = jnp.sum(value * value, axis=1, keepdims=True) * (1.0 / emb)
            out_ref[...] = value * lax.rsqrt(mean_square + 1e-06)

        @pl.when(c == 0)
        def _():
            pairs = [units_of(RS_XL)[q] for q in (1, 2, 3, 4, 0)]
            count = len(pairs)

            def slot(j, i):
                return ((y + j) % NY) * 2 + (x + i) % 2

            def x_first(b, n):
                k = b * 3 + n
                return copy(x1_s.at[k], x1_r.at[k], rs_s, rs_r.at[k], x_next)

            def diagonal(n):
                d = pairs.index((RS_XL[n], 0)) % 2
                to = dev(z + STEP[d], y, 1 - x, 0)
                return copy(x1_s.at[n], x1_r.at[n], rs_s, rs_r.at[n], to)

            def compute(b, carry):
                odd = b % 2
                off = odd * ((7 - b) // 2) - (1 - odd) * ((8 - b) // 2)
                zz = (z + 16 + off) % NZ
                unit(zz, trans[zz, :, :, 0], trans_peer[zz])
                for n, j in enumerate(RS_XL):
                    x1_s[b * 3 + n] = part[zz, slot(j, 1)].astype(BF)
                return carry

            def compute_send(b, carry):
                compute(b, carry)
                for n in range(len(RS_XL)):
                    x_first(b, n).start()
                return carry

            def ring(d, s, u):
                k = spot(d, s, u)
                return copy(big_s.at[k], big_r.at[k], rs_s, rs_r.at[24 + k], dev(z + STEP[d], y, x, 0))

            def spot(d, s, u):
                return u if s == 1 else count + (s - 2) * 2 * count + d * count + u

            def local(b, u):
                j, i = pairs[u]
                value = part[(z + RS_OFFS[b]) % NZ, slot(j, i)]
                if j in RS_XL and b:
                    n = RS_XL.index(j)
                    x_first(b, n).wait_recv()
                    value = value + x1_r[b * 3 + n].astype(F32)
                return value

            def first(u):
                d = u % 2
                big_s[spot(d, 1, u)] = local(0, u).astype(BF)
                ring(d, 1, u).start()

            compute(0, 0)
            for u in range(count):
                first(u)
            for n in range(len(RS_XL)):
                diagonal(n).start()
            lax.fori_loop(1, NZ, compute_send, 0)
            for s in range(2, 5):
                for u in range(count):
                    for d in range(2):
                        value = local(2 * s - 3 + d, u)
                        if s > 2 or u % 2 == d:
                            ring(d, s - 1, u).wait_recv()
                            value = value + big_r[spot(d, s - 1, u)].astype(F32)
                        if s == 2 and u % 2 == d and pairs[u][0] in RS_XL:
                            n = RS_XL.index(pairs[u][0])
                            diagonal(n).wait_recv()
                            value = value + x1_r[n].astype(F32)
                        big_s[spot(d, s, u)] = value.astype(BF)
                        ring(d, s, u).start()

            def last(j, i):
                k = j * 2 + i
                n = 24 + 7 * count + pairs.index((j, i))
                return copy(fin_s.at[k], fin_r.at[k], rs_s, rs_r.at[n], dev(z, y + j, (x + i) % 2, 0))

            for u in range(count):
                j, i = pairs[u]
                value = local(7, u)
                for d in range(2):
                    ring(d, 4, u).wait_recv()
                    value = value + big_r[spot(d, 4, u)].astype(F32)
                if u < count - 1:
                    fin_s[j * 2 + i] = value.astype(BF)
                    last(j, i).start()
                else:
                    total[0] = value
            value = total[0]
            for j, i in pairs[-2::-1]:
                last(j, i).wait_recv()
                value = value + fin_r[j * 2 + i].astype(F32)
            finish(value)
            sent(big_s.at[pl.ds(0, 24 + 8 * count - 1)], rs_s, rs_r.at[0])

        @pl.when(c == 1)
        def _():
            def compute(i, carry):
                yy = (y + 2 + i // 2) % NY
                h = i % 2
                half = pl.ds(h * 4, 4)
                unit(yy * 2 + h, trans[half, yy, :, 1], trans_peer[half, yy])
                return carry

            def local(yy, j):
                zz = (z + RS_OFFS[j]) % NZ
                return part[(yy % NY) * 2 + zz // 4, pl.ds((zz % 4) * 2, 2)]

            def ring(d, s, j):
                k = spot(d, s, j)
                span = pl.ds(2 * k, 2)
                to = dev(z, y + (2 if s == 1 and j == 0 else STEP[d]), x, 1)
                return copy(big_s.at[span], big_r.at[span], rs_s, rs_r.at[k], to)

            def spot(d, s, j):
                return j if s == 1 else 8 + d * 8 + j

            def place(d, s, j):
                return pl.ds(2 * spot(d, s, j), 2)

            lax.fori_loop(0, 2, compute, 0)
            for j in range(8):
                big_s[place(j % 2, 1, j)] = local(y + 2, j).astype(BF)
                ring(j % 2, 1, j).start()
            lax.fori_loop(2, NZ, compute, 0)
            for j in range(8):
                for d in range(2):
                    value = local(y + STEP[d], j)
                    if j and j % 2 == d:
                        ring(d, 1, j).wait_recv()
                        value = value + big_r[place(d, 1, j)].astype(F32)
                    big_s[place(d, 2, j)] = value.astype(BF)
                    ring(d, 2, j).start()

            def landed(j):
                if j == 0:
                    ring(0, 1, 0).wait_recv()
                for d in range(2):
                    ring(d, 2, j).wait_recv()

            def piece(j, i):
                zz = (z + RS_OFFS[j]) % NZ
                side = (x + i) % 2
                value = part[y * 2 + zz // 4, (zz % 4) * 2 + side]
                if j == 0:
                    value = value + big_r[side].astype(F32)
                for d in range(2):
                    value = value + big_r[2 * spot(d, 2, j) + side].astype(F32)
                return value

            def ring2(d, s, i):
                k = (s - 1) * 2 + i
                to = dev(z + STEP[d], y, (x + (i if s == 4 else 0)) % 2, 1)
                return copy(small_s.at[d, k], small_r.at[d, k], rs_s, rs_r.at[24 + d * 8 + k], to)

            landed(0)
            for i in range(2):
                small_s[i, i] = piece(0, i).astype(BF)
                ring2(i, 1, i).start()
            for s in range(2, 5):
                for d in range(2):
                    landed(2 * s - 3 + d)
                    for i in (1, 0):
                        k = (s - 1) * 2 + i
                        value = piece(2 * s - 3 + d, i)
                        if s > 2 or i == d:
                            ring2(d, s - 1, i).wait_recv()
                            value = value + small_r[d, k - 2].astype(F32)
                        small_s[d, k] = value.astype(BF)
                        ring2(d, s, i).start()
            landed(7)
            fin_s[0] = piece(7, 1).astype(BF)
            last = copy(fin_s.at[0], fin_r.at[0], rs_s, rs_r.at[40], x_next)
            last.start()
            value = piece(7, 0)
            for d in range(2):
                for i in range(2):
                    ring2(d, 4, i).wait_recv()
                    value = value + small_r[d, 6 + i].astype(F32)
            last.wait_recv()
            finish(value + fin_r[0].astype(F32))
            sent(big_s.at[pl.ds(0, 63)], rs_s, rs_r.at[0])

        turned_copy().wait_send()


def shards(token_states, token_ids, master, gain, cand_ids, slab_owner):
    seqs, length, width = token_states.shape[1:]
    tokens = seqs * length
    rows, emb = master.shape[1:]
    vmem = pl.BlockSpec(memory_space=pltpu.VMEM)
    smem = pl.BlockSpec(memory_space=pltpu.SMEM)
    hbm = pl.BlockSpec(memory_space=pl.ANY)
    dma = pltpu.SemaphoreType.DMA
    V = pltpu.VMEM
    out = pl.pallas_call(
        body,
        out_shape=jax.ShapeDtypeStruct((rows, emb), F32),
        in_specs=[hbm, hbm, hbm, vmem, vmem, smem, smem],
        out_specs=vmem,
        scratch_shapes=[
            V((tokens, width), BF),
            V((rows, emb), F32),
            V((1, width), F32),
            V((tokens, width), BF),
            V((NZ, NY, 2, 2, rows, tokens), BF),
            V((NZ, NY, 2, rows, tokens), BF),
            V((NZ, NY, 2, 2, rows, emb), BF),
            V((rows, emb), BF),
            V((tokens, emb), F32),
            V((3, 8, emb // 8), F32),
            V((3, 8, emb // 8), BF),
            V((NZ, NY, 2, 2, 3, 8, emb // 8), BF),
            V((tokens, emb), BF),
            V((tokens, emb), BF),
            V((tokens, emb), F32),
            V((seqs, 1, length), jnp.int32),
            V((3, 8, emb // 8), F32),
            V((NZ, 8, rows, emb), F32),
            V((2, rows, emb), F32),
            V((64, rows, emb), BF),
            V((64, rows, emb), BF),
            V((24, rows, emb), BF),
            V((24, rows, emb), BF),
            V((2, 8, rows, emb), BF),
            V((2, 8, rows, emb), BF),
            V((8, rows, emb), BF),
            V((8, rows, emb), BF),
            pltpu.SMEM((24,), jnp.int32),
            dma((3,)),
            dma, dma((64,)),
            dma, dma,
            dma, dma,
            dma, dma,
            dma, dma((3,)),
            dma, dma((8,)),
            dma, dma,
            dma, dma,
            dma((2,)), dma((2,)),
            dma, dma((64,)),
        ],
        compiler_params=pltpu.CompilerParams(
            collective_id=0, has_side_effects=True, vmem_limit_bytes=62 * 1024 * 1024
        ),
    )(
        token_states.reshape(tokens, width),
        master[0],
        gain.reshape(1, width),
        token_ids.reshape(seqs, 1, length),
        slab_owner.reshape(3, -1),
        cand_ids,
        slab_owner,
    )
    return out[None]


def solution(mesh):
    placed = (
        P("grp", "fsdp", None, None),
        P("grp", "fsdp", None),
        P("grp", "fsdp", None),
        P(),
        P("fsdp", None),
        P(),
    )
    return jax.shard_map(
        shards, mesh=mesh, in_specs=placed, out_specs=P("grp", "fsdp", None), check_vma=False
    )
```
